32 devices in a mesh: groups: 2 (over y), shots: 4 (over z), dom: 2 (over x), sub: 2 (over core).
Axes of the slice: x: 2, y: 2, z: 4, core: 2. Of those that a mesh axis runs over, the one named last changes fastest.
Arguments:
- velocity: float32 [64, 16, 256], P(('groups', 'shots'), 'dom', 'sub'), parts along dimension 0, may hold values from 0.15 to 0.4
- wave_prev: bfloat16 [8, 32, 16, 256], P(('groups', 'shots'), None, 'dom', 'sub'), parts along dimension 0, may hold values from -6 to 6
- wave_now: bfloat16 [8, 32, 16, 256], P(('groups', 'shots'), None, 'dom', 'sub'), parts along dimension 0, may hold values from -6 to 6
- adj_next: bfloat16 [8, 32, 16, 256], P(('groups', 'shots'), None, 'dom', 'sub'), parts along dimension 0, may hold values from -6 to 6
- adj_now: bfloat16 [8, 32, 16, 256], P(('groups', 'shots'), None, 'dom', 'sub'), parts along dimension 0, may hold values from -6 to 6
- sponge: int32 [32, 16, 256], P(None, 'dom', 'sub'), may hold values 0 or 1
- wavelet: float32 [8, 6], P(('groups', 'shots')), parts along dimension 0, may hold values from -12 to 12
- src_pos: int32 [8], P(('groups', 'shots')), parts along dimension 0, may hold values from 0 to 4095
- rec_pos: int32 [8, 256], P(('groups', 'shots')), parts along dimension 0, may hold values from 0 to 4095
- observed: float32 [8, 4, 256], P(('groups', 'shots')), parts along dimension 0, may hold values from -6 to 6
Outputs:
- direction: float32 [64, 16, 256], P(('groups', 'shots'), 'dom', 'sub'), parts along dimension 0
- wave_out: float32 [8, 32, 16, 256], P(('groups', 'shots'), None, 'dom', 'sub'), parts along dimension 0
The draws below stay inside these ranges and needn't reach their ends.
There are 2 independent parts, one for each index of `groups`. The reference program is written for one: setup_inputs(seed, part) draws one part's arguments, and reference() takes and returns one part's arrays. A program takes and returns all parts, laid end to end along the dimension named above; an argument that names none is the same for every part. Nothing has to cross between parts.
Inputs may be any that keep to these rules, and one draw needn't show every extreme that they name: `src_pos`: a horizontal position x * 256 + y on the grid. `rec_pos`: horizontal positions x * 256 + y on the grid, possibly repeated.
All inputs are finite; a program needn't handle non-finite values. Where the reference program divides by a largest or mean magnitude, that divisor is 1e-20 or more. No bound on the sum of `sponge` on one device may be relied on, other than what follows from the above.
Results may differ from the reference program's by a relative error of at most 0.0003.
Values sent between devices are 32-bit elements; how exact they have to be, the bound alone decides.
A program may use at most 64 MiB of HBM per device.

```python
import math
import jax
import jax.numpy as jnp
from jax import lax

NZ = 32
NREC = 256
NF = 4
NFIN = 2
SHOTS = 4
NX = 16
NY = 256


def touch_ends(result, stream_key, smallest, largest):
    longest = result.shape.index(max(result.shape))
    spots = []
    for shift in (0, 1):
        where = [jax.random.randint(jax.random.fold_in(stream_key, axis), (), 0, length) for axis, length in enumerate(result.shape)]
        where[longest] = (where[longest] + shift) % result.shape[longest]
        spots.append(tuple(where))
    return result.at[spots[0]].set(smallest).at[spots[1]].set(largest)


def steps_of(key, shape, split, low, top_value):
    level, own = 1.0, jax.random.fold_in(key, 6)
    for dim, blocks in split:
        draws = jnp.exp(jax.random.uniform(jax.random.fold_in(own, dim), (blocks,), jnp.float32, low / len(split), top_value / len(split)))
        level = level * jnp.repeat(draws, shape[dim] // blocks).reshape([-1 if axis == dim else 1 for axis in range(len(shape))])
    return level


def bell_draw(own_key, shape, spread, most, pieces=(), dtype=jnp.bfloat16):
    array = jax.random.normal(own_key, shape, jnp.float32) * spread
    if len(pieces) > 0:
        array = steps_of(own_key, shape, pieces, -0.22, 0.18) * array
    return jnp.clip(array, min=-most, max=most).astype(dtype)


def setup_inputs(seed: int = 0, part: int = 0) -> dict:
    keys = jax.random.split(jax.random.key(seed), 11)
    part_splits = jax.random.split(jax.random.fold_in(keys[10], part), 11)
    return {
        "velocity": jnp.clip(jnp.exp(math.log(0.4) - 0.98082923 * jax.random.uniform(part_splits[0], (NZ, NX, NY), jnp.float32) ** steps_of(part_splits[0], (NZ, NX, NY), ((0, 4), (1, 2), (2, 2)), -0.2, 0.2)), 0.15, 0.4),
        "wave_prev": bell_draw(part_splits[1], (SHOTS, NZ, NX, NY), 1.0, 6.0, ((0, 4), (2, 2), (3, 2))),
        "wave_now": bell_draw(part_splits[2], (SHOTS, NZ, NX, NY), 1.0, 6.0, ((0, 4), (2, 2), (3, 2))),
        "adj_next": bell_draw(part_splits[3], (SHOTS, NZ, NX, NY), 1.0, 6.0, ((0, 4), (2, 2), (3, 2))),
        "adj_now": bell_draw(part_splits[4], (SHOTS, NZ, NX, NY), 1.0, 6.0, ((0, 4), (2, 2), (3, 2))),
        "sponge": touch_ends((jax.random.randint(keys[5], (NZ, NX, NY), 0, 4) < 1).astype(jnp.int32), jax.random.fold_in(keys[5], 1), 0, 1),
        "wavelet": bell_draw(part_splits[6], (SHOTS, NF + NFIN), 3.0, 12.0, ((0, 4),), jnp.float32),
        "src_pos": touch_ends(jax.random.randint(part_splits[7], (SHOTS,), 0, NX * NY), jax.random.fold_in(part_splits[7], 1), 0, (NX * NY) - 1).astype(jnp.int32),
        "rec_pos": touch_ends(jax.random.randint(part_splits[8], (SHOTS, NREC), 0, NX * NY), jax.random.fold_in(part_splits[8], 1), 0, (NX * NY) - 1).astype(jnp.int32),
        "observed": bell_draw(part_splits[9], (SHOTS, NF, NREC), 1.0, 6.0, ((0, 4),), jnp.float32),
    }


coeffs = (-205.0 / 72.0, 8.0 / 5.0, -1.0 / 5.0, 8.0 / 315.0, -1.0 / 560.0)
damp_rate = 0.2
step_rate = 0.1
floor_share = 0.5
src_depth = 2
rec_depth = 1
reach = 4


def laplace(padded, depth, rows, cols):
    z0, x0, y0 = reach, reach, reach
    total = (3.0 * coeffs[0]) * padded[z0:z0 + depth, x0:x0 + rows, y0:y0 + cols]
    for offset in range(1, 5):
        pair = padded[z0 + offset:z0 + offset + depth, x0:x0 + rows, y0:y0 + cols]
        pair = pair + padded[z0 - offset:z0 - offset + depth, x0:x0 + rows, y0:y0 + cols]
        pair = pair + padded[z0:z0 + depth, x0 + offset:x0 + offset + rows, y0:y0 + cols]
        pair = pair + padded[z0:z0 + depth, x0 - offset:x0 - offset + rows, y0:y0 + cols]
        pair = pair + padded[z0:z0 + depth, x0:x0 + rows, y0 + offset:y0 + offset + cols]
        pair = pair + padded[z0:z0 + depth, x0:x0 + rows, y0 - offset:y0 - offset + cols]
        total = total + coeffs[offset] * pair
    return total


def advance(now, before, kappa, damp, plane, level):
    padded = jnp.pad(now, reach)
    lap = laplace(padded, now.shape[0], now.shape[1], now.shape[2])
    numer = 2.0 * now - (1.0 - damp) * before + kappa * lap
    numer = numer.at[level].add(plane)
    return numer / (1.0 + damp)


def place(positions, values):
    flat = jnp.zeros((NX * NY,), jnp.float32).at[positions].add(values)
    return flat.reshape(NX, NY)


def forward(prev, now, kappa, damp, amps, spot):
    states = [prev.astype(jnp.float32), now.astype(jnp.float32)]
    for step in range(NF):
        plane = place(spot[None], amps[step][None])
        states.append(advance(states[-1], states[-2], kappa, damp, plane, src_depth))
    return states


def reference(velocity, wave_prev, wave_now, adj_next, adj_now, sponge, wavelet, src_pos, rec_pos, observed):
    kappa = velocity * velocity
    damp = damp_rate * sponge.astype(jnp.float32)

    def one_shot(carry, items):
        grad_total, illum_total = carry
        prev, now, lam_after, lam_now, amps, spot, receivers, recorded = items
        states = forward(prev, now, kappa, damp, amps, spot)
        lam_after = lam_after.astype(jnp.float32)
        lam_now = lam_now.astype(jnp.float32)
        grad = jnp.zeros_like(kappa)
        for level in range(NF, 0, -1):
            trace = states[level + 1][rec_depth].reshape(-1)[receivers]
            resid = trace - recorded[level - 1]
            plane = place(receivers, resid)
            lam_before = advance(lam_now, lam_after, kappa, damp, plane, rec_depth)
            lower = level - 1
            accel = states[lower + 2] - 2.0 * states[lower + 1] + states[lower]
            grad = grad + lam_before * accel
            lam_after, lam_now = lam_now, lam_before
        illum = jnp.zeros_like(kappa)
        for level in range(1, NF + 1):
            illum = illum + states[level + 1] * states[level + 1]
        return (grad_total + grad, illum_total + illum), None

    zeros = jnp.zeros_like(kappa)
    (gradient, illumination), _ = lax.scan(one_shot, (zeros, zeros),
                                           (wave_prev, wave_now, adj_next, adj_now, wavelet, src_pos, rec_pos, observed))
    precond = gradient / (illumination + floor_share * SHOTS)
    peak = jnp.max(jnp.abs(precond))
    direction = precond / (peak + 1e-6)
    updated = velocity * (1.0 - step_rate * direction)
    kappa_new = updated * updated

    def final_shot(items):
        prev, now, amps, spot = items
        states = forward(prev, now, kappa, damp, amps, spot)
        before, current = states[-2], states[-1]
        for step in range(NFIN):
            plane = place(spot[None], amps[NF + step][None])
            nxt = advance(current, before, kappa_new, damp, plane, src_depth)
            before, current = current, nxt
        return current

    wave_out = lax.map(final_shot, (wave_prev, wave_now, wavelet, src_pos))
    return direction, wave_out
```

```python
import functools

import jax
import jax.numpy as jnp
import numpy as np
from jax import lax
from jax.experimental import pallas as pl
from jax.experimental.pallas import tpu as pltpu
from jax.sharding import PartitionSpec as P

VM_MAIN = 48 * 1024 * 1024
VM_PART = 2 * 1024 * 1024
NF = 4
NFIN = 2

coeffs = (-205.0 / 72.0, 8.0 / 5.0, -1.0 / 5.0, 8.0 / 315.0, -1.0 / 560.0)
damp_rate = 0.2
step_rate = 0.1
floor_share = 0.5
src_depth = 2
rec_depth = 1
reach = 4
unit = coeffs[1]
centre = 3.0 * coeffs[0] / unit

MESH = pl.DeviceIdType.MESH
F32 = jnp.float32
BF16 = jnp.bfloat16


def along_y(size):
    full = np.zeros((size, size), np.float32)
    for row in range(size):
        for k in range(1, reach + 1):
            for col in (row - k, row + k):
                if 0 <= col < size:
                    full[row, col] = coeffs[k] / unit
    return full.astype(BF16)


def along_zx(zb, X):
    full = np.zeros((zb, X, zb + 2 * reach, X), np.float32)
    for z in range(zb):
        for x in range(X):
            for k in range(1, reach + 1):
                for other in (-k, k):
                    full[z, x, z + reach + other, x] = coeffs[k] / unit
                    if 0 <= x + other < X:
                        full[z, x, z + reach, x + other] = coeffs[k] / unit
    return full.reshape(zb * X, (zb + 2 * reach) * X).astype(BF16)


def split(value):
    high = value.astype(BF16)
    low = (value - high.astype(F32)).astype(BF16)
    return high, low


def copies_needed(shots, dom, sub):
    fields = 5 * ((dom - 1) + dom * (sub - 1))
    slab = shots * dom * sub
    back = (shots * dom - 1) + shots * (sub - 1) + (sub - 1)
    return fields + slab + 2 * (shots - 1) + back


def kernel(
    sizes,
    vel_in, prev_in, now_in, adjn_in, adj_in, sponge_in, amp_in, src_ref, rec_in, obs_in, ym_in, zx_in,
    both_ref,
    vel_ref, prev_ref, now_ref, adjn_ref, adj_ref, sponge_ref, amp_ref, rec_ref, obs_ref, ym_ref, zx_ref,
    U, L, H, V, SP, IV, KP, ACC, PC, PK, OB, CNT, SR, GI, GR, ss, rs, ls,
):
    shots, dom, sub, depth, rows, cols, owned, zb = sizes
    X, Y = dom * rows, sub * cols
    s = lax.axis_index("shots")
    d = lax.axis_index("dom")
    c = lax.axis_index("sub")
    counts = {"shots": shots, "dom": dom, "sub": sub}
    me = {"shots": s, "dom": d, "sub": c}
    tickets = [0]
    sent = []

    def peer(axis, j):
        return lax.rem(me[axis] + j, counts[axis])

    def source(axis, j):
        return lax.rem(me[axis] + (counts[axis] - j), counts[axis])

    def xs(i):
        return pl.ds(pl.multiple_of(i * rows, rows), rows)

    def ys(i):
        return pl.ds(pl.multiple_of(i * cols, cols), cols)

    def send_to(src, dst, shifts):
        idx = tickets[0]
        tickets[0] += 1
        copy = pltpu.make_async_remote_copy(
            src_ref=src, dst_ref=dst, send_sem=ss.at[idx], recv_sem=rs.at[idx],
            device_id={axis: peer(axis, j) for axis, j in shifts.items() if j}, device_id_type=MESH,
        )
        copy.start()
        sent.append(copy)
        return idx

    def send(src, dst, axis, j):
        return send_to(src, dst, {axis: j})

    def arrived(idx, dst, axis):
        pltpu.make_async_remote_copy(
            src_ref=dst, dst_ref=dst, send_sem=ss.at[idx], recv_sem=rs.at[idx],
            device_id={axis: peer(axis, 1)}, device_id_type=MESH,
        ).wait_recv()

    def field_send(place):
        hops = [(i, send(place(d, c), place(d, c), "dom", i)) for i in range(1, dom)]
        cross = [(0, k, send(place(d, c), place(d, c), "sub", k)) for k in range(1, sub)]
        return hops, cross

    def field_relay(place, state):
        hops, cross = state
        for i, idx in hops:
            here = place(source("dom", i), c)
            arrived(idx, here, "dom")
            cross += [(i, k, send(here, here, "sub", k)) for k in range(1, sub)]

    def field_done(place, state):
        for i, k, idx in state[1]:
            arrived(idx, place(source("dom", i), source("sub", k)), "sub")

    def slab_send(place, first, second):
        own = place({"shots": s, "dom": d}, c)
        state = {
            "one": [(i, send(own, own, first, i)) for i in range(1, counts[first])],
            "two": [(0, j, send(own, own, second, j)) for j in range(1, counts[second])],
            "cross": [(0, 0, k, send(own, own, "sub", k)) for k in range(1, sub)],
        }
        return state

    def slab_relay(place, state, first, second):
        for i, idx in state["one"]:
            here = place({first: source(first, i), second: me[second]}, c)
            arrived(idx, here, first)
            state["two"] += [(i, j, send(here, here, second, j)) for j in range(1, counts[second])]
            state["cross"] += [(i, 0, k, send(here, here, "sub", k)) for k in range(1, sub)]

    def slab_relay_two(place, state, first, second):
        for i, j, idx in state["two"]:
            here = place({first: source(first, i), second: source(second, j)}, c)
            arrived(idx, here, second)
            state["cross"] += [(i, j, k, send(here, here, "sub", k)) for k in range(1, sub)]

    def slab_done(place, state, first, second):
        for i, j, k, idx in state["cross"]:
            arrived(idx, place({first: source(first, i), second: source(second, j)}, source("sub", k)), "sub")

    def in_field(ref, n):
        return lambda i, k: ref.at[n, :, xs(i), ys(k)]

    def in_whole(ref):
        return lambda i, k: ref.at[:, xs(i), ys(k)]

    def in_slab(ref):
        return lambda at, k: ref.at[pl.ds(at["shots"] * owned, owned), xs(at["dom"]), ys(k)]

    def neighbours(slot, b, exact, lanes=slice(None)):
        lo = b * zb
        acc = None
        for part_of in (0,) if exact else (0, 1):
            near = H[slot, part_of, lo : lo + zb + 2 * reach, :, lanes].reshape((zb + 2 * reach) * X, -1)
            mid = H[slot, part_of, lo + reach : lo + reach + zb].reshape(zb * X, Y)
            term = jnp.dot(zx_ref[...], near, preferred_element_type=F32)
            acc = term if acc is None else acc + term
            acc = acc + jnp.dot(mid, ym_ref[:, lanes], preferred_element_type=F32)
        return acc.reshape(zb, X, -1)

    def keep(slot, z, value, exact=False):
        high = value.astype(BF16)
        H[slot, 0, reach + z] = high
        if not exact:
            H[slot, 1, reach + z] = (value - high.astype(F32)).astype(BF16)

    def amp_at(n):
        return amp_ref[0, n]

    blocks = depth // zb
    barrier = pltpu.get_barrier_semaphore()
    greeted = 0
    for axis, count in counts.items():
        for j in range(1, count):
            pl.semaphore_signal(barrier, inc=1, device_id={axis: peer(axis, j)}, device_id_type=MESH)
            greeted += 1
    for i in range(1, dom):
        for j in range(1, shots):
            pl.semaphore_signal(
                barrier, inc=1, device_id={"shots": peer("shots", j), "dom": peer("dom", i)}, device_id_type=MESH
            )
            greeted += 1

    loads = {}
    for place, source_ref, target in (
        (0, vel_in, vel_ref), (1, now_in, now_ref), (2, sponge_in, sponge_ref), (3, prev_in, prev_ref),
        (4, adj_in, adj_ref), (5, adjn_in, adjn_ref), (6, rec_in, rec_ref), (7, obs_in, obs_ref),
        (8, amp_in, amp_ref), (9, ym_in, ym_ref), (10, zx_in, zx_ref),
    ):
        loads[place] = pltpu.make_async_copy(source_ref, target, ls.at[place])
        loads[place].start()

    own_x, own_y = xs(d), ys(c)
    for z in range(depth):
        PC[z] = jnp.zeros((X, Y), F32)
    loads[0].wait()
    V[pl.ds(s * owned, owned), own_x, own_y] = vel_ref[...]
    loads[1].wait()
    U[1, :, own_x, own_y] = now_ref[0].astype(F32)

    pl.semaphore_wait(barrier, greeted)

    vel_state = slab_send(in_slab(V), "dom", "shots")
    now_state = field_send(in_field(U, 1))
    loads[2].wait()
    SP[:, own_x, own_y] = sponge_ref[...].astype(F32)
    sp_state = field_send(in_whole(SP))
    loads[3].wait()
    U[0, :, own_x, own_y] = prev_ref[0].astype(F32)
    prev_state = field_send(in_field(U, 0))
    loads[4].wait()
    L[1, :, own_x, own_y] = adj_ref[0].astype(F32)
    adj_state = field_send(in_field(L, 1))
    loads[5].wait()
    L[0, :, own_x, own_y] = adjn_ref[0].astype(F32)
    adjn_state = field_send(in_field(L, 0))
    for place in range(6, 11):
        loads[place].wait()

    edge = jnp.zeros((reach, X, Y), BF16)
    for slot in range(H.shape[0]):
        for part_of in range(2):
            H[slot, part_of, 0:reach] = edge
            H[slot, part_of, reach + depth : 2 * reach + depth] = edge
    pos = rec_ref[...]
    row_of = jnp.zeros_like(pos)
    for x in range(1, X):
        row_of = row_of + (pos >= x * Y).astype(jnp.int32)
    col_of = pos - row_of * Y
    nrec = pos.shape[1]
    x_hot = (lax.broadcasted_iota(jnp.int32, (X, nrec), 0) == row_of).astype(F32)
    y_hot = (lax.broadcasted_iota(jnp.int32, (Y, nrec), 0) == col_of).astype(F32).astype(BF16)

    def spread(lhs):
        return lax.dot_general(lhs, y_hot, (((1,), (1,)), ((), ())), preferred_element_type=F32)

    CNT[...] = spread(x_hot.astype(BF16))
    slab_relay(in_slab(V), vel_state, "dom", "shots")
    for n in range(NF):
        vals = x_hot * obs_ref[0, n : n + 1, :]
        a = vals.astype(BF16)
        b, rest = split(vals - a.astype(F32))
        OB[n] = spread(a) + spread(b) + spread(rest)
    flat = lax.broadcasted_iota(jnp.int32, (X, Y), 0) * Y + lax.broadcasted_iota(jnp.int32, (X, Y), 1)
    src_hot = (flat == src_ref[0]).astype(F32)

    field_relay(in_field(U, 1), now_state)
    field_relay(in_whole(SP), sp_state)
    field_done(in_field(U, 1), now_state)
    for z in range(depth):
        keep(0, z, U[1, z], True)
    for b in range(blocks):
        ACC[b * zb : (b + 1) * zb] = neighbours(0, b, True)
    slab_relay_two(in_slab(V), vel_state, "dom", "shots")
    field_relay(in_field(U, 0), prev_state)
    slab_done(in_slab(V), vel_state, "dom", "shots")
    field_done(in_whole(SP), sp_state)
    for z in range(depth):
        inv = 1.0 / (1.0 + damp_rate * SP[z])
        IV[z] = 2.0 * inv
        vel = V[z]
        KP[z] = vel * vel * (unit * inv)
    field_done(in_field(U, 0), prev_state)

    def carried(ref, n, z, xr, yr):
        before = ref[n - 1, z, xr, yr]
        return IV[z, xr, yr] * (ref[n, z, xr, yr] - before) + before

    whole_x, whole_y = slice(None), slice(None)

    def advance(ref, n, slot, plane, at, ready=False):
        for b in range(blocks):
            acc = None if ready else neighbours(slot, b, False)
            for i in range(zb):
                z = b * zb + i
                lap = (ACC[z] if ready else acc[i]) + centre * ref[n, z]
                value = carried(ref, n, z, whole_x, whole_y) + KP[z] * lap
                if z == at:
                    value = value + IV[z] * plane
                ref[n + 1, z] = value
                keep(slot ^ 1, z, value)

    for n in range(NF):
        advance(U, n + 1, n % 2, src_hot * (0.5 * amp_at(n)), src_depth, n == 0)
        if n == max(0, NF - 2):
            field_relay(in_field(L, 1), adj_state)

    for z in range(depth):
        illum = None
        for n in range(NF):
            value = U[n + 2, z, own_x, own_y]
            illum = value * value if illum is None else illum + value * value
        GI[1, z] = illum
    field_done(in_field(L, 1), adj_state)
    for z in range(depth):
        keep(2, z, L[1, z], True)
    for b in range(blocks):
        ACC[b * zb : (b + 1) * zb] = neighbours(2, b, True)
    field_relay(in_field(L, 0), adjn_state)
    far_first = sorted(range(1, shots), key=lambda j: -min(j, shots - j))

    def to_owners(f):
        return [
            (j, send(GI.at[f, pl.ds(peer("shots", j) * owned, owned)], GR.at[j - 1, f], "shots", j))
            for j in far_first
        ]

    illum_parts = to_owners(1)
    field_done(in_field(L, 0), adjn_state)

    def plane_of(n):
        return 0.5 * (CNT[...] * U[n + 1, rec_depth] - OB[n - 1])

    for n in range(NF, 1, -1):
        advance(L, NF + 1 - n, 2 + (NF - n) % 2, plane_of(n), rec_depth, n == NF)

    last = NF
    for b in range(blocks):
        ACC[b * zb : (b + 1) * zb, :, 0:cols] = neighbours(2 + (NF - 1) % 2, b, False, own_y)
    SR[0] = plane_of(1)
    source_plane = SR[0, own_x, own_y]
    for z in range(depth):
        lap = ACC[z, own_x, 0:cols] + centre * L[last, z, own_x, own_y]
        lam = carried(L, last, z, own_x, own_y) + KP[z, own_x, own_y] * lap
        if z == rec_depth:
            lam = lam + IV[z, own_x, own_y] * source_plane
        u = [U[n, z, own_x, own_y] for n in range(NF + 2)]
        grad = lam * (u[2] - 2.0 * u[1] + u[0])
        for n in range(1, NF):
            grad = grad + L[NF + 1 - n, z, own_x, own_y] * (u[n + 2] - 2.0 * u[n + 1] + u[n])
        GI[0, z] = grad

    grad_parts = to_owners(0)
    plane = src_hot * (0.5 * amp_at(NF))
    for b in range(blocks):
        acc = neighbours(NF % 2, b, False)
        for i in range(zb):
            z = b * zb + i
            value = carried(U, NF + 1, z, whole_x, whole_y)
            if z == src_depth:
                value = value + IV[z] * plane
            U[NF + 2, z] = value
            ACC[z] = KP[z] * (acc[i] + centre * U[NF + 1, z])
    below = GI[1, pl.ds(s * owned, owned)] + floor_share * shots
    for j, idx in illum_parts:
        arrived(idx, GR.at[j - 1, 1], "shots")
        below = below + GR[j - 1, 1]
    above = GI[0, pl.ds(s * owned, owned)]
    for j, idx in grad_parts:
        arrived(idx, GR.at[j - 1, 0], "shots")
        above = above + GR[j - 1, 0]
    mine = above / below
    PC[pl.ds(s * owned, owned), own_x, own_y] = mine
    slab = in_slab(PC)
    own = slab(me, c)
    column = [(j, send(own, own, "shots", j)) for j in far_first]
    beside = [
        (i, j, send_to(own, own, {"dom": i, "shots": j})) for i in range(1, dom) for j in far_first + [0]
    ]
    cross = [(0, k, send(own, own, "sub", k)) for k in range(1, sub)]
    for j, idx in reversed(column):
        here = slab({"shots": source("shots", j), "dom": d}, c)
        arrived(idx, here, "shots")
        cross += [(j, k, send(here, here, "sub", k)) for k in range(1, sub)]
    for i, j, idx in reversed(beside):
        arrived(idx, slab({"shots": source("shots", j), "dom": source("dom", i)}, c), "dom")
    top = jnp.abs(PC[0, :, own_y])
    for z in range(1, depth):
        top = jnp.maximum(top, jnp.abs(PC[z, :, own_y]))
    PK[0] = top
    peaks = [(k, send(PK.at[0], PK.at[k], "sub", k)) for k in range(1, sub)]
    for j, k, idx in cross:
        arrived(idx, slab({"shots": source("shots", j), "dom": d}, source("sub", k)), "sub")
    for k, idx in peaks:
        arrived(idx, PK.at[k], "sub")
        top = jnp.maximum(top, PK[k])
    peak = jnp.max(jnp.max(top, axis=0, keepdims=True), axis=1, keepdims=True)
    scale = 1.0 / (peak + 1e-06)
    both_ref[0:owned] = mine * scale
    rate = step_rate * scale
    slot = (NF + 1) % 2
    for z in range(depth):
        factor = 1.0 - rate * PC[z]
        factor = factor * factor
        value = U[NF + 2, z] + ACC[z] * factor
        U[NF + 2, z] = value
        keep(slot, z, value)
    for b in range(blocks):
        ACC[b * zb : (b + 1) * zb, :, 0:cols] = neighbours(slot, b, False, own_y)
    SR[1] = src_hot * (0.5 * amp_at(NF + 1))
    for z in range(depth):
        lap = ACC[z, own_x, 0:cols] + centre * U[NF + 2, z, own_x, own_y]
        factor = 1.0 - rate * PC[z, own_x, own_y]
        value = carried(U, NF + 2, z, own_x, own_y) + KP[z, own_x, own_y] * (factor * factor) * lap
        if z == src_depth:
            value = value + IV[z, own_x, own_y] * SR[1, own_x, own_y]
        both_ref[owned + z] = value
    for copy in sent:
        copy.wait_send()


def part(both_ref, dir_ref, out_ref):
    owned = dir_ref.shape[0]
    dir_ref[...] = both_ref[0:owned]
    out_ref[0] = both_ref[owned:]


def solution(mesh):
    shots, dom, sub = mesh.shape["shots"], mesh.shape["dom"], mesh.shape["sub"]

    def shards(velocity, wave_prev, wave_now, adj_next, adj_now, sponge, wavelet, src_pos, rec_pos, observed):
        depth, rows, cols = sponge.shape
        owned = velocity.shape[0]
        X, Y = dom * rows, sub * cols
        zb = min(depth, max(1, 128 // X))
        ym = along_y(Y)
        zx = along_zx(zb, X)
        vm = pl.BlockSpec(memory_space=pltpu.VMEM)
        hbm = pl.BlockSpec(memory_space=pltpu.HBM)
        sm = pl.BlockSpec(memory_space=pltpu.SMEM)
        operands = (
            velocity, wave_prev, wave_now, adj_next, adj_now, sponge, wavelet, src_pos, rec_pos, observed,
            jnp.asarray(ym), jnp.asarray(zx),
        )
        whole = pltpu.VMEM((depth, X, Y), F32)
        n_sems = copies_needed(shots, dom, sub)
        both = pl.pallas_call(
            functools.partial(kernel, (shots, dom, sub, depth, rows, cols, owned, zb)),
            out_shape=jax.ShapeDtypeStruct((owned + depth, rows, cols), F32),
            in_specs=[sm if a.ndim == 1 else hbm for a in operands],
            out_specs=vm,
            scratch_shapes=[(pltpu.SMEM if a.size < 128 else pltpu.VMEM)(a.shape, a.dtype) for a in operands if a.ndim > 1] + [
                pltpu.VMEM((NF + 3, depth, X, Y), F32),
                pltpu.VMEM((NF + 1, depth, X, Y), F32),
                pltpu.VMEM((4, 2, depth + 2 * reach, X, Y), BF16),
                whole, whole, whole, whole, whole, whole,
                pltpu.VMEM((sub, X, cols), F32),
                pltpu.VMEM((NF, X, Y), F32),
                pltpu.VMEM((X, Y), F32),
                pltpu.VMEM((2, X, Y), F32),
                pltpu.VMEM((2, depth, rows, cols), F32),
                pltpu.VMEM((max(1, shots - 1), 2, owned, rows, cols), F32),
                pltpu.SemaphoreType.DMA((n_sems,)),
                pltpu.SemaphoreType.DMA((n_sems,)),
                pltpu.SemaphoreType.DMA((len(operands) - 1,)),
            ],
            compiler_params=pltpu.CompilerParams(
                collective_id=0, has_side_effects=True, vmem_limit_bytes=VM_MAIN
            ),
        )(*(pltpu.with_memory_space_constraint(a, pltpu.HBM) if a.ndim > 1 else a for a in operands))
        return tuple(pl.pallas_call(
            part,
            out_shape=(
                jax.ShapeDtypeStruct((owned, rows, cols), F32),
                jax.ShapeDtypeStruct((1, depth, rows, cols), F32),
            ),
            in_specs=[vm],
            out_specs=(vm, vm),
            compiler_params=pltpu.CompilerParams(vmem_limit_bytes=VM_PART),
        )(both))

    return jax.shard_map(
        shards,
        mesh=mesh,
        in_specs=(
            P(("groups", "shots"), "dom", "sub"),
            P(("groups", "shots"), None, "dom", "sub"),
            P(("groups", "shots"), None, "dom", "sub"),
            P(("groups", "shots"), None, "dom", "sub"),
            P(("groups", "shots"), None, "dom", "sub"),
            P(None, "dom", "sub"),
            P(("groups", "shots"), None),
            P(("groups", "shots")),
            P(("groups", "shots"), None),
            P(("groups", "shots"), None, None),
        ),
        out_specs=(
            P(("groups", "shots"), "dom", "sub"),
            P(("groups", "shots"), None, "dom", "sub"),
        ),
        check_vma=False,
    )
```

```python
import functools

import jax
import jax.numpy as jnp
import numpy as np
from jax import lax
from jax.experimental import pallas as pl
from jax.experimental.pallas import tpu as pltpu
from jax.sharding import PartitionSpec as P

VM_MAIN = 48 * 1024 * 1024
VM_PART = 2 * 1024 * 1024
NF = 4
NFIN = 2

coeffs = (-205.0 / 72.0, 8.0 / 5.0, -1.0 / 5.0, 8.0 / 315.0, -1.0 / 560.0)
damp_rate = 0.2
step_rate = 0.1
floor_share = 0.5
src_depth = 2
rec_depth = 1
reach = 4
unit = coeffs[1]
centre = 3.0 * coeffs[0] / unit

MESH = pl.DeviceIdType.MESH
F32 = jnp.float32
BF16 = jnp.bfloat16


def along_y(size):
    full = np.zeros((size, size), np.float32)
    for row in range(size):
        for k in range(1, reach + 1):
            for col in (row - k, row + k):
                if 0 <= col < size:
                    full[row, col] = coeffs[k] / unit
    return full.astype(BF16)


def along_zx(zb, X):
    full = np.zeros((zb, X, zb + 2 * reach, X), np.float32)
    for z in range(zb):
        for x in range(X):
            for k in range(1, reach + 1):
                for other in (-k, k):
                    full[z, x, z + reach + other, x] = coeffs[k] / unit
                    if 0 <= x + other < X:
                        full[z, x, z + reach, x + other] = coeffs[k] / unit
    return full.reshape(zb * X, (zb + 2 * reach) * X).astype(BF16)


def split(value):
    high = value.astype(BF16)
    low = (value - high.astype(F32)).astype(BF16)
    return high, low


def copies_needed(parts, shots, dom, sub):
    fields = 4 * ((dom - 1) + dom * (sub - 1))
    mask = (dom - 1) * (1 + (parts - 1)) + (1 + (dom - 1) * parts) * (sub - 1)
    slab = shots * dom * sub
    back = (shots - 1) + (dom - 1) * shots * sub + shots * (sub - 1)
    return fields + mask + slab + 2 * (shots - 1) + back


def kernel(
    sizes,
    vel_in, prev_in, now_in, adjn_in, adj_in, sponge_in, amp_in, src_ref, rec_in, obs_in, ym_in, zx_in,
    both_ref,
    prev_ref, now_ref, adjn_ref, adj_ref, amp_ref, rec_ref, obs_ref, ym_ref, zx_ref,
    U, L, H, V, SP, IV, KP, ACC, PC, HS, HR, CR, OB, CNT, SR, GI, GR, ss, rs, ls,
):
    parts, shots, dom, sub, depth, rows, cols, owned, zb = sizes
    X, Y = dom * rows, sub * cols
    s = lax.axis_index("shots")
    d = lax.axis_index("dom")
    c = lax.axis_index("sub")
    g = lax.axis_index("groups") if parts > 1 else 0
    counts = {"groups": parts, "shots": shots, "dom": dom, "sub": sub}
    me = {"groups": g, "shots": s, "dom": d, "sub": c}
    tickets = [0]
    sent = []

    def peer(axis, j):
        return lax.rem(me[axis] + j, counts[axis])

    def source(axis, j):
        return lax.rem(me[axis] + (counts[axis] - j), counts[axis])

    def xs(i):
        return pl.ds(pl.multiple_of(i * rows, rows), rows)

    def ys(i):
        return pl.ds(pl.multiple_of(i * cols, cols), cols)

    def send_to(src, dst, shifts):
        idx = tickets[0]
        tickets[0] += 1
        copy = pltpu.make_async_remote_copy(
            src_ref=src, dst_ref=dst, send_sem=ss.at[idx], recv_sem=rs.at[idx],
            device_id={axis: peer(axis, j) for axis, j in shifts.items() if j}, device_id_type=MESH,
        )
        copy.start()
        sent.append(copy)
        return idx

    def send(src, dst, axis, j):
        return send_to(src, dst, {axis: j})

    def arrived(idx, dst, axis):
        pltpu.make_async_remote_copy(
            src_ref=dst, dst_ref=dst, send_sem=ss.at[idx], recv_sem=rs.at[idx],
            device_id={axis: peer(axis, 1)}, device_id_type=MESH,
        ).wait_recv()

    def field_send(place):
        hops = [(i, send(place(d, c), place(d, c), "dom", i)) for i in range(1, dom)]
        cross = [(0, k, send(place(d, c), place(d, c), "sub", k)) for k in range(1, sub)]
        return hops, cross

    def field_relay(place, state):
        hops, cross = state
        for i, idx in hops:
            here = place(source("dom", i), c)
            arrived(idx, here, "dom")
            cross += [(i, k, send(here, here, "sub", k)) for k in range(1, sub)]

    def field_done(place, state):
        for i, k, idx in state[1]:
            arrived(idx, place(source("dom", i), source("sub", k)), "sub")

    def slab_send(place, own, first, second):
        there = place({"shots": s, "dom": d}, c)
        return {
            "one": [(i, send(own, there, first, i)) for i in range(1, counts[first])],
            "two": [(0, j, send(own, there, second, j)) for j in range(1, counts[second])],
            "cross": [(0, 0, k, send(own, there, "sub", k)) for k in range(1, sub)],
        }

    def slab_relay(place, state, first, second):
        for i, idx in state["one"]:
            here = place({first: source(first, i), second: me[second]}, c)
            arrived(idx, here, first)
            state["two"] += [(i, j, send(here, here, second, j)) for j in range(1, counts[second])]
            state["cross"] += [(i, 0, k, send(here, here, "sub", k)) for k in range(1, sub)]

    def slab_relay_two(place, state, first, second, which):
        for i, j, idx in state["two"]:
            if (i == 0) == which:
                here = place({first: source(first, i), second: source(second, j)}, c)
                arrived(idx, here, second)
                state["cross"] += [(i, j, k, send(here, here, "sub", k)) for k in range(1, sub)]

    def slab_done(place, state, first, second):
        for i, j, k, idx in state["cross"]:
            arrived(idx, place({first: source(first, i), second: source(second, j)}, source("sub", k)), "sub")

    def in_field(ref, n):
        return lambda i, k: ref.at[n, :, xs(i), ys(k)]

    def in_whole(ref):
        return lambda i, k: ref.at[:, xs(i), ys(k)]

    def in_slab(ref):
        return lambda at, k: ref.at[pl.ds(at["shots"] * owned, owned), xs(at["dom"]), ys(k)]

    def neighbours(slot, b, exact, lanes=slice(None)):
        lo = b * zb
        acc = None
        for part_of in (0,) if exact else (0, 1):
            near = H[slot, part_of, lo : lo + zb + 2 * reach, :, lanes].reshape((zb + 2 * reach) * X, -1)
            mid = H[slot, part_of, lo + reach : lo + reach + zb].reshape(zb * X, Y)
            term = jnp.dot(zx_ref[...], near, preferred_element_type=F32)
            acc = term if acc is None else acc + term
            acc = acc + jnp.dot(mid, ym_ref[:, lanes], preferred_element_type=F32)
        return acc.reshape(zb, X, -1)

    def keep(slot, z, value, exact=False):
        high = value.astype(BF16)
        H[slot, 0, reach + z] = high
        if not exact:
            H[slot, 1, reach + z] = (value - high.astype(F32)).astype(BF16)

    def amp_at(n):
        return amp_ref[0, n]

    blocks = depth // zb
    barrier = pltpu.get_barrier_semaphore()
    greeted = 0
    shifts = [{"dom": i, "sub": k, "shots": j} for j in range(shots) for i in range(dom) for k in range(sub)][1:]
    for shift in [{"groups": j} for j in range(1, parts)] + shifts:
        pl.semaphore_signal(
            barrier, inc=1, device_id={axis: peer(axis, j) for axis, j in shift.items() if j}, device_id_type=MESH
        )
        greeted += 1

    own_x, own_y = xs(d), ys(c)
    own_slab = in_slab(V)({"shots": s, "dom": d}, c)
    loads = []
    for source_ref, target in (
        (now_in, now_ref), (prev_in, prev_ref), (adj_in, adj_ref), (adjn_in, adjn_ref),
        (vel_in, own_slab), (sponge_in, SP.at[:, own_x, own_y]),
        (rec_in, rec_ref), (obs_in, obs_ref), (amp_in, amp_ref), (ym_in, ym_ref), (zx_in, zx_ref),
    ):
        loads.append(pltpu.make_async_copy(source_ref, target, ls.at[len(loads)]))
        loads[-1].start()
    loads[0].wait()
    U[1, :, own_x, own_y] = now_ref[0].astype(F32)

    pl.semaphore_wait(barrier, greeted)

    share = depth // parts

    def piece(part_at):
        return pl.ds(pl.multiple_of(part_at * share, share), share)

    vel_state = slab_send(in_slab(V), vel_in, "dom", "shots")
    mask_state = [(i, send(sponge_in.at[piece(g)], SP.at[piece(g), own_x, own_y], "dom", i)) for i in range(1, dom)]
    now_state = field_send(in_field(U, 1))
    mask_cross = [
        (SP.at[:, own_x, ys(source("sub", k))], send(sponge_in, SP.at[:, own_x, own_y], "sub", k)) for k in range(1, sub)
    ]
    loads[1].wait()
    U[0, :, own_x, own_y] = prev_ref[0].astype(F32)
    prev_state = field_send(in_field(U, 0))
    loads[2].wait()
    L[1, :, own_x, own_y] = adj_ref[0].astype(F32)
    adj_state = field_send(in_field(L, 1))
    loads[3].wait()
    L[0, :, own_x, own_y] = adjn_ref[0].astype(F32)
    adjn_state = field_send(in_field(L, 0))
    for z in range(depth):
        PC[z] = jnp.zeros((X, Y), F32)
    for load in loads[4:]:
        load.wait()

    def mask_pass(part_at, i, idx, axis):
        there = xs(source("dom", i))
        here = SP.at[piece(part_at), there, own_y]
        arrived(idx, here, axis)
        for k in range(1, sub):
            mask_cross.append((SP.at[piece(part_at), there, ys(source("sub", k))], send(here, here, "sub", k)))
        return here

    edge = jnp.zeros((reach, X, Y), BF16)
    for slot in range(H.shape[0]):
        for part_of in range(2):
            H[slot, part_of, 0:reach] = edge
            H[slot, part_of, reach + depth : 2 * reach + depth] = edge
    pos = rec_ref[...]
    row_of = jnp.zeros_like(pos)
    for x in range(1, X):
        row_of = row_of + (pos >= x * Y).astype(jnp.int32)
    col_of = pos - row_of * Y
    nrec = pos.shape[1]
    x_hot = (lax.broadcasted_iota(jnp.int32, (X, nrec), 0) == row_of).astype(F32)
    y_hot = (lax.broadcasted_iota(jnp.int32, (Y, nrec), 0) == col_of).astype(F32).astype(BF16)

    def spread(lhs):
        return lax.dot_general(lhs, y_hot, (((1,), (1,)), ((), ())), preferred_element_type=F32)

    CNT[...] = spread(x_hot.astype(BF16))
    slab_relay(in_slab(V), vel_state, "dom", "shots")
    mask_far = []
    for i, idx in mask_state:
        here = mask_pass(g, i, idx, "dom")
        mask_far += [(i, j, send(here, here, "groups", j)) for j in range(1, parts)]
    slab_relay_two(in_slab(V), vel_state, "dom", "shots", True)
    for n in range(NF):
        vals = x_hot * obs_ref[0, n : n + 1, :]
        a = vals.astype(BF16)
        b, rest = split(vals - a.astype(F32))
        OB[n] = spread(a) + spread(b) + spread(rest)
    flat = lax.broadcasted_iota(jnp.int32, (X, Y), 0) * Y + lax.broadcasted_iota(jnp.int32, (X, Y), 1)
    src_hot = (flat == src_ref[0]).astype(F32)

    field_relay(in_field(U, 1), now_state)
    field_done(in_field(U, 1), now_state)
    for z in range(depth):
        keep(0, z, U[1, z], True)
    for b in range(blocks):
        ACC[b * zb : (b + 1) * zb] = neighbours(0, b, True)
    slab_relay_two(in_slab(V), vel_state, "dom", "shots", False)
    for i, j, idx in mask_far:
        mask_pass(source("groups", j), i, idx, "groups")
    field_relay(in_field(U, 0), prev_state)
    slab_done(in_slab(V), vel_state, "dom", "shots")
    for here, idx in mask_cross:
        arrived(idx, here, "sub")
    for z in range(depth):
        twice = 2.0 - (2.0 - 2.0 / (1.0 + damp_rate)) * SP[z].astype(F32)
        IV[z] = twice
        vel = V[z]
        KP[z] = vel * vel * (0.5 * unit * twice)
    field_done(in_field(U, 0), prev_state)

    def carried(ref, n, z, xr, yr):
        before = ref[n - 1, z, xr, yr]
        return IV[z, xr, yr] * (ref[n, z, xr, yr] - before) + before

    whole_x, whole_y = slice(None), slice(None)

    def advance(ref, n, slot, plane, at, ready=False):
        for b in range(blocks):
            acc = None if ready else neighbours(slot, b, False)
            for i in range(zb):
                z = b * zb + i
                lap = (ACC[z] if ready else acc[i]) + centre * ref[n, z]
                value = carried(ref, n, z, whole_x, whole_y) + KP[z] * lap
                if z == at:
                    value = value + IV[z] * plane
                ref[n + 1, z] = value
                keep(slot ^ 1, z, value)

    for n in range(NF):
        advance(U, n + 1, n % 2, src_hot * (0.5 * amp_at(n)), src_depth, n == 0)
        if n == max(0, NF - 2):
            field_relay(in_field(L, 1), adj_state)

    for z in range(depth):
        illum = None
        for n in range(NF):
            value = U[n + 2, z, own_x, own_y]
            illum = value * value if illum is None else illum + value * value
        GI[1, z] = illum
    field_done(in_field(L, 1), adj_state)
    for z in range(depth):
        keep(2, z, L[1, z], True)
    for b in range(blocks):
        ACC[b * zb : (b + 1) * zb] = neighbours(2, b, True)
    field_relay(in_field(L, 0), adjn_state)
    far_first = sorted(range(1, shots), key=lambda j: -min(j, shots - j))

    def to_owners(f):
        return [
            (j, send(GI.at[f, pl.ds(peer("shots", j) * owned, owned)], GR.at[j - 1, f], "shots", j))
            for j in far_first
        ]

    illum_parts = to_owners(1)
    field_done(in_field(L, 0), adjn_state)

    def plane_of(n):
        return 0.5 * (CNT[...] * U[n + 1, rec_depth] - OB[n - 1])

    for n in range(NF, 1, -1):
        advance(L, NF + 1 - n, 2 + (NF - n) % 2, plane_of(n), rec_depth, n == NF)

    last = NF
    for b in range(blocks):
        ACC[b * zb : (b + 1) * zb, :, 0:cols] = neighbours(2 + (NF - 1) % 2, b, False, own_y)
    SR[0] = plane_of(1)
    source_plane = SR[0, own_x, own_y]
    for z in range(depth):
        lap = ACC[z, own_x, 0:cols] + centre * L[last, z, own_x, own_y]
        lam = carried(L, last, z, own_x, own_y) + KP[z, own_x, own_y] * lap
        if z == rec_depth:
            lam = lam + IV[z, own_x, own_y] * source_plane
        u = [U[n, z, own_x, own_y] for n in range(NF + 2)]
        grad = lam * (u[2] - 2.0 * u[1] + u[0])
        for n in range(1, NF):
            grad = grad + L[NF + 1 - n, z, own_x, own_y] * (u[n + 2] - 2.0 * u[n + 1] + u[n])
        GI[0, z] = grad

    grad_parts = to_owners(0)
    plane = src_hot * (0.5 * amp_at(NF))
    for b in range(blocks):
        acc = neighbours(NF % 2, b, False)
        for i in range(zb):
            z = b * zb + i
            value = carried(U, NF + 1, z, whole_x, whole_y)
            if z == src_depth:
                value = value + IV[z] * plane
            U[NF + 2, z] = value
            ACC[z] = KP[z] * (acc[i] + centre * U[NF + 1, z])
    below = GI[1, pl.ds(s * owned, owned)] + floor_share * shots
    for j, idx in illum_parts:
        arrived(idx, GR.at[j - 1, 1], "shots")
        below = below + GR[j - 1, 1]
    above = GI[0, pl.ds(s * owned, owned)]
    for j, idx in grad_parts:
        arrived(idx, GR.at[j - 1, 0], "shots")
        above = above + GR[j - 1, 0]
    mine = above / below
    PC[pl.ds(s * owned, owned), own_x, own_y] = mine
    slab = in_slab(PC)
    own = slab(me, c)
    most = jnp.max(jnp.abs(mine), axis=0)
    most = functools.reduce(jnp.maximum, [most[r : r + reach] for r in range(0, rows, reach)])
    for i in range(1, dom):
        HS[i - 1, 0:owned] = jnp.where(peer("dom", i) > d, mine[:, rows - reach : rows], mine[:, 0:reach])
        HS[i - 1, owned] = most
    column, beside, corner = [], [], []
    for j in far_first + [0]:
        if j:
            column.append((j, send(own, own, "shots", j)))
        for i in range(1, dom):
            beside.append((i, j, send_to(HS.at[i - 1], HR.at[i - 1, s], {"dom": i, "shots": j})))
            for k in range(1, sub):
                corner.append((
                    i, j, k,
                    send_to(HS.at[i - 1, owned], CR.at[i - 1, k - 1, s], {"dom": i, "shots": j, "sub": k}),
                ))
    cross = [(0, k, send(own, own, "sub", k)) for k in range(1, sub)]
    for j, idx in reversed(column):
        here = slab({"shots": source("shots", j), "dom": d}, c)
        arrived(idx, here, "shots")
        cross += [(j, k, send(here, here, "sub", k)) for k in range(1, sub)]
    top = jnp.abs(PC[0, own_x, own_y])
    for z in range(1, depth):
        top = jnp.maximum(top, jnp.abs(PC[z, own_x, own_y]))
    for i, j, k, idx in reversed(corner):
        arrived(idx, CR.at[i - 1, k - 1, source("shots", j)], "dom")
    for i, j, idx in reversed(beside):
        arrived(idx, HR.at[i - 1, source("shots", j)], "dom")
    rest = None
    for i in range(1, dom):
        across = xs(source("dom", i))
        for z in range(depth):
            halo = HR[i - 1, z // owned, z % owned]
            PC[z, across, own_y] = jnp.concatenate([halo] * (rows // reach), axis=0)
        for j in range(shots):
            values = [HR[i - 1, j, owned]] + [CR[i - 1, k - 1, j] for k in range(1, sub)]
            for value in values:
                rest = value if rest is None else jnp.maximum(rest, value)
    for j, k, idx in cross:
        arrived(idx, slab({"shots": source("shots", j), "dom": d}, source("sub", k)), "sub")
    for k in range(1, sub):
        for z in range(depth):
            top = jnp.maximum(top, jnp.abs(PC[z, own_x, ys(source("sub", k))]))
    if rest is not None:
        top = jnp.concatenate([top, rest], axis=0)
    peak = jnp.max(jnp.max(top, axis=0, keepdims=True), axis=1, keepdims=True)
    scale = 1.0 / (peak + 1e-06)
    both_ref[0:owned] = mine * scale
    rate = step_rate * scale
    slot = (NF + 1) % 2
    for z in range(depth):
        factor = 1.0 - rate * PC[z]
        factor = factor * factor
        value = U[NF + 2, z] + ACC[z] * factor
        U[NF + 2, z] = value
        keep(slot, z, value)
    for b in range(blocks):
        ACC[b * zb : (b + 1) * zb, :, 0:cols] = neighbours(slot, b, False, own_y)
    SR[1] = src_hot * (0.5 * amp_at(NF + 1))
    for z in range(depth):
        lap = ACC[z, own_x, 0:cols] + centre * U[NF + 2, z, own_x, own_y]
        factor = 1.0 - rate * PC[z, own_x, own_y]
        value = carried(U, NF + 2, z, own_x, own_y) + KP[z, own_x, own_y] * (factor * factor) * lap
        if z == src_depth:
            value = value + IV[z, own_x, own_y] * SR[1, own_x, own_y]
        both_ref[owned + z] = value
    for copy in sent:
        copy.wait_send()


def part(both_ref, dir_ref, out_ref):
    owned = dir_ref.shape[0]
    dir_ref[...] = both_ref[0:owned]
    out_ref[0] = both_ref[owned:]


def solution(mesh):
    shots, dom, sub = mesh.shape["shots"], mesh.shape["dom"], mesh.shape["sub"]
    parts = mesh.shape["groups"]

    def shards(velocity, wave_prev, wave_now, adj_next, adj_now, sponge, wavelet, src_pos, rec_pos, observed):
        depth, rows, cols = sponge.shape
        owned = velocity.shape[0]
        X, Y = dom * rows, sub * cols
        zb = min(depth, max(1, 128 // X))
        ym = along_y(Y)
        zx = along_zx(zb, X)
        vm = pl.BlockSpec(memory_space=pltpu.VMEM)
        hbm = pl.BlockSpec(memory_space=pltpu.HBM)
        sm = pl.BlockSpec(memory_space=pltpu.SMEM)
        operands = (
            velocity, wave_prev, wave_now, adj_next, adj_now, sponge, wavelet, src_pos, rec_pos, observed,
            jnp.asarray(ym), jnp.asarray(zx),
        )
        whole = pltpu.VMEM((depth, X, Y), F32)
        share = parts if depth % parts == 0 else 1
        n_sems = copies_needed(share, shots, dom, sub)
        both = pl.pallas_call(
            functools.partial(kernel, (share, shots, dom, sub, depth, rows, cols, owned, zb)),
            out_shape=jax.ShapeDtypeStruct((owned + depth, rows, cols), F32),
            in_specs=[sm if a.ndim == 1 else hbm for a in operands],
            out_specs=vm,
            scratch_shapes=[
                (pltpu.SMEM if a.size < 128 else pltpu.VMEM)(a.shape, a.dtype)
                for a in operands if a.ndim > 1 and a is not velocity and a is not sponge
            ] + [
                pltpu.VMEM((NF + 3, depth, X, Y), F32),
                pltpu.VMEM((NF + 1, depth, X, Y), F32),
                pltpu.VMEM((4, 2, depth + 2 * reach, X, Y), BF16),
                whole, pltpu.VMEM((depth, X, Y), jnp.int32), whole, whole, whole, whole,
                pltpu.VMEM((max(1, dom - 1), owned + 1, reach, cols), F32),
                pltpu.VMEM((max(1, dom - 1), shots, owned + 1, reach, cols), F32),
                pltpu.VMEM((max(1, dom - 1), max(1, sub - 1), shots, reach, cols), F32),
                pltpu.VMEM((NF, X, Y), F32),
                pltpu.VMEM((X, Y), F32),
                pltpu.VMEM((2, X, Y), F32),
                pltpu.VMEM((2, depth, rows, cols), F32),
                pltpu.VMEM((max(1, shots - 1), 2, owned, rows, cols), F32),
                pltpu.SemaphoreType.DMA((n_sems,)),
                pltpu.SemaphoreType.DMA((n_sems,)),
                pltpu.SemaphoreType.DMA((len(operands) - 1,)),
            ],
            compiler_params=pltpu.CompilerParams(
                collective_id=0, has_side_effects=True, vmem_limit_bytes=VM_MAIN
            ),
        )(*(pltpu.with_memory_space_constraint(a, pltpu.HBM) if a.ndim > 1 else a for a in operands))
        return tuple(pl.pallas_call(
            part,
            out_shape=(
                jax.ShapeDtypeStruct((owned, rows, cols), F32),
                jax.ShapeDtypeStruct((1, depth, rows, cols), F32),
            ),
            in_specs=[vm],
            out_specs=(vm, vm),
            compiler_params=pltpu.CompilerParams(vmem_limit_bytes=VM_PART),
        )(both))

    return jax.shard_map(
        shards,
        mesh=mesh,
        in_specs=(
            P(("groups", "shots"), "dom", "sub"),
            P(("groups", "shots"), None, "dom", "sub"),
            P(("groups", "shots"), None, "dom", "sub"),
            P(("groups", "shots"), None, "dom", "sub"),
            P(("groups", "shots"), None, "dom", "sub"),
            P(None, "dom", "sub"),
            P(("groups", "shots"), None),
            P(("groups", "shots")),
            P(("groups", "shots"), None),
            P(("groups", "shots"), None, None),
        ),
        out_specs=(
            P(("groups", "shots"), "dom", "sub"),
            P(("groups", "shots"), None, "dom", "sub"),
        ),
        check_vma=False,
    )
```

```python
import functools

import jax
import jax.numpy as jnp
import numpy as np
from jax import lax
from jax.experimental import pallas as pl
from jax.experimental.pallas import tpu as pltpu
from jax.sharding import PartitionSpec as P

VM_MAIN = 48 * 1024 * 1024
VM_PART = 2 * 1024 * 1024
NF = 4
NFIN = 2

coeffs = (-205.0 / 72.0, 8.0 / 5.0, -1.0 / 5.0, 8.0 / 315.0, -1.0 / 560.0)
damp_rate = 0.2
step_rate = 0.1
floor_share = 0.5
src_depth = 2
rec_depth = 1
reach = 4
unit = coeffs[1]
centre = 3.0 * coeffs[0] / unit

MESH = pl.DeviceIdType.MESH
F32 = jnp.float32
BF16 = jnp.bfloat16


def along_y(size):
    full = np.zeros((size, size), np.float32)
    for row in range(size):
        for k in range(1, reach + 1):
            for col in (row - k, row + k):
                if 0 <= col < size:
                    full[row, col] = coeffs[k] / unit
    return full.astype(BF16)


def along_zx(zb, X):
    full = np.zeros((zb, X, zb + 2 * reach, X), np.float32)
    for z in range(zb):
        for x in range(X):
            for k in range(1, reach + 1):
                for other in (-k, k):
                    full[z, x, z + reach + other, x] = coeffs[k] / unit
                    if 0 <= x + other < X:
                        full[z, x, z + reach, x + other] = coeffs[k] / unit
    return full.reshape(zb * X, (zb + 2 * reach) * X).astype(BF16)


def split(value):
    high = value.astype(BF16)
    low = (value - high.astype(F32)).astype(BF16)
    return high, low


N_SEMS = 22


def kernel(
    sizes,
    vel_in, prev_in, now_in, adjn_in, adj_in, sponge_in, amp_in, src_ref, rec_in, obs_in, ym_in, zx_in,
    both_ref,
    prev_ref, now_ref, adjn_ref, adj_ref, amp_ref, rec_ref, obs_ref, ym_ref, zx_ref,
    U, L, H, V, SP, IV, KP, ACC, PC, HS, HR, CR, OB, CNT, SR, GI, GR, ss, rs, ls,
):
    parts, shots, dom, sub, depth, rows, cols, owned, zb, sharing = sizes
    X, Y = dom * rows, sub * cols
    s = lax.axis_index("shots")
    d = lax.axis_index("dom")
    c = lax.axis_index("sub")
    g = lax.axis_index("groups")
    counts = {"groups": parts, "shots": shots, "dom": dom, "sub": sub}
    me = {"groups": g, "shots": s, "dom": d, "sub": c}
    groups = []

    def peer(axis, j):
        return lax.rem(me[axis] + j, counts[axis])

    def source(axis, j):
        return lax.rem(me[axis] + (counts[axis] - j), counts[axis])

    def xs(i):
        return pl.ds(pl.multiple_of(i * rows, rows), rows)

    def ys(i):
        return pl.ds(pl.multiple_of(i * cols, cols), cols)

    def group(total):
        groups.append(total)
        return len(groups) - 1

    def put(idx, src, dst, shifts):
        pltpu.make_async_remote_copy(
            src_ref=src, dst_ref=dst, send_sem=ss.at[idx], recv_sem=rs.at[idx],
            device_id={axis: peer(axis, j) for axis, j in shifts.items() if j}, device_id_type=MESH,
        ).start()

    def whole_group(idx):
        return pltpu.make_async_remote_copy(
            src_ref=groups[idx], dst_ref=groups[idx], send_sem=ss.at[idx], recv_sem=rs.at[idx],
            device_id={"sub": peer("sub", 1)}, device_id_type=MESH,
        )

    def take(idx):
        whole_group(idx).wait_recv()

    def put_sub(idx, src, dst):
        for k in range(1, sub):
            put(idx, src, dst, {"sub": k})

    far_cols, far_rows = pl.ds(0, (sub - 1) * cols), pl.ds(0, (dom - 1) * rows)

    def field_send(ref, n):
        state = group(ref.at[n, :, far_rows, 0:cols]), group(ref.at[n, :, :, far_cols])
        here = ref.at[n, :, xs(d), ys(c)]
        for i in range(1, dom):
            put(state[0], here, here, {"dom": i})
        put_sub(state[1], here, here)
        return state

    def field_relay(ref, n, state):
        take(state[0])
        for i in range(1, dom):
            here = ref.at[n, :, xs(source("dom", i)), ys(c)]
            put_sub(state[1], here, here)

    def in_slab(ref):
        return lambda at, k: ref.at[pl.ds(at["shots"] * owned, owned), xs(at["dom"]), ys(k)]

    def neighbours(slot, b, exact, lanes=slice(None)):
        lo = b * zb
        acc = None
        for part_of in (0,) if exact else (0, 1):
            near = H[slot, part_of, lo : lo + zb + 2 * reach, :, lanes].reshape((zb + 2 * reach) * X, -1)
            mid = H[slot, part_of, lo + reach : lo + reach + zb].reshape(zb * X, Y)
            term = jnp.dot(zx_ref[...], near, preferred_element_type=F32)
            acc = term if acc is None else acc + term
            acc = acc + jnp.dot(mid, ym_ref[:, lanes], preferred_element_type=F32)
        return acc.reshape(zb, X, -1)

    def keep(slot, z, value, exact=False):
        high = value.astype(BF16)
        H[slot, 0, reach + z] = high
        if not exact:
            H[slot, 1, reach + z] = (value - high.astype(F32)).astype(BF16)

    def amp_at(n):
        return amp_ref[0, n]

    blocks = depth // zb
    barrier = pltpu.get_barrier_semaphore()
    greeted = 0
    shifts = [{"shots": j, "dom": i, "sub": k} for j in range(shots) for i in range(dom) for k in range(sub)][1:]
    sharers = [{"groups": i, "shots": j} for j in range(shots) for i in range(parts if sharing > shots else 1)][1:sharing]
    for shift in [shift for shift in sharers if shift["groups"]] + shifts:
        pl.semaphore_signal(
            barrier, inc=1, device_id={axis: peer(axis, j) for axis, j in shift.items() if j}, device_id_type=MESH
        )
        greeted += 1

    own_x, own_y = xs(d), ys(c)
    own_slab = in_slab(V)({"shots": s, "dom": d}, c)
    loads = []
    for source_ref, target in (
        (now_in, now_ref), (prev_in, prev_ref), (adj_in, adj_ref), (adjn_in, adjn_ref),
        (vel_in, own_slab), (sponge_in, SP.at[:, own_x, own_y]),
        (rec_in, rec_ref), (obs_in, obs_ref), (amp_in, amp_ref), (ym_in, ym_ref), (zx_in, zx_ref),
    ):
        loads.append(pltpu.make_async_copy(source_ref, target, ls.at[len(loads)]))
        loads[-1].start()

    pl.semaphore_wait(barrier, greeted)

    share = depth // sharing
    mine_at = pl.ds(pl.multiple_of((g * shots + s if sharing > shots else s) * share, share), share) if sharing > 1 else slice(None)
    slab = in_slab(V)
    vel_across = group(V.at[0:owned, far_rows, 0:cols])
    vel_near = group(V.at[pl.ds(0, (shots - 1) * owned), 0:rows, 0:cols])
    vel_far = group(V.at[pl.ds(0, (shots - 1) * owned), far_rows, 0:cols])
    vel_cross = group(V.at[:, :, far_cols])
    mask_across = group(SP.at[0:share, far_rows, 0:cols])
    mask_far = group(SP.at[pl.ds(0, (sharing - 1) * share), far_rows, 0:cols]) if sharing > 1 else None
    mask_cross = group(SP.at[:, :, far_cols])
    for i in range(1, dom):
        put(vel_across, vel_in, own_slab, {"dom": i})
        put(mask_across, sponge_in.at[mine_at], SP.at[mine_at, own_x, own_y], {"dom": i})
    for j in range(1, shots):
        put(vel_near, vel_in, own_slab, {"shots": j})
    loads[0].wait()
    U[1, :, own_x, own_y] = now_ref[0].astype(F32)
    now_state = field_send(U, 1)
    put_sub(vel_cross, vel_in, own_slab)
    put_sub(mask_cross, sponge_in, SP.at[:, own_x, own_y])
    loads[1].wait()
    U[0, :, own_x, own_y] = prev_ref[0].astype(F32)
    prev_state = field_send(U, 0)
    loads[2].wait()
    L[1, :, own_x, own_y] = adj_ref[0].astype(F32)
    adj_state = field_send(L, 1)
    loads[3].wait()
    L[0, :, own_x, own_y] = adjn_ref[0].astype(F32)
    adjn_state = field_send(L, 0)
    for z in range(depth):
        PC[z] = jnp.zeros((X, Y), F32)
    for load in loads[4:]:
        load.wait()

    edge = jnp.zeros((reach, X, Y), BF16)
    for slot in range(H.shape[0]):
        for part_of in range(2):
            H[slot, part_of, 0:reach] = edge
            H[slot, part_of, reach + depth : 2 * reach + depth] = edge
    pos = rec_ref[...]
    row_of = jnp.zeros_like(pos)
    for x in range(1, X):
        row_of = row_of + (pos >= x * Y).astype(jnp.int32)
    col_of = pos - row_of * Y
    nrec = pos.shape[1]
    x_hot = (lax.broadcasted_iota(jnp.int32, (X, nrec), 0) == row_of).astype(F32)
    y_hot = (lax.broadcasted_iota(jnp.int32, (Y, nrec), 0) == col_of).astype(F32).astype(BF16)

    def spread(lhs):
        return lax.dot_general(lhs, y_hot, (((1,), (1,)), ((), ())), preferred_element_type=F32)

    CNT[...] = spread(x_hot.astype(BF16))
    take(vel_across)
    for i in range(1, dom):
        here = slab({"shots": s, "dom": source("dom", i)}, c)
        for j in range(1, shots):
            put(vel_far, here, here, {"shots": j})
        put_sub(vel_cross, here, here)
    take(mask_across)
    for i in range(1, dom):
        here = SP.at[mine_at, xs(source("dom", i)), own_y]
        for shift in sharers:
            put(mask_far, here, here, shift)
    take(vel_near)
    for j in range(1, shots):
        here = slab({"shots": source("shots", j), "dom": d}, c)
        put_sub(vel_cross, here, here)
    for n in range(NF):
        vals = x_hot * obs_ref[0, n : n + 1, :]
        a = vals.astype(BF16)
        b, rest = split(vals - a.astype(F32))
        OB[n] = spread(a) + spread(b) + spread(rest)
    flat = lax.broadcasted_iota(jnp.int32, (X, Y), 0) * Y + lax.broadcasted_iota(jnp.int32, (X, Y), 1)
    src_hot = (flat == src_ref[0]).astype(F32)

    field_relay(U, 1, now_state)
    take(now_state[1])
    for z in range(depth):
        keep(0, z, U[1, z], True)
    for b in range(blocks):
        ACC[b * zb : (b + 1) * zb] = neighbours(0, b, True)
    take(vel_far)
    for i in range(1, dom):
        for j in range(1, shots):
            here = slab({"shots": source("shots", j), "dom": source("dom", i)}, c)
            put_sub(vel_cross, here, here)
    field_relay(U, 0, prev_state)
    if sharing > 1:
        take(mask_far)
    for i in range(1, dom):
        here = SP.at[:, xs(source("dom", i)), own_y]
        put_sub(mask_cross, here, here)
    take(vel_cross)
    take(mask_cross)
    for z in range(depth):
        twice = 2.0 - (2.0 - 2.0 / (1.0 + damp_rate)) * SP[z].astype(F32)
        IV[z] = twice
        vel = V[z]
        KP[z] = vel * vel * (0.5 * unit * twice)
    take(prev_state[1])

    def carried(ref, n, z, xr, yr):
        before = ref[n - 1, z, xr, yr]
        return IV[z, xr, yr] * (ref[n, z, xr, yr] - before) + before

    whole_x, whole_y = slice(None), slice(None)

    def advance(ref, n, slot, plane, at, ready=False):
        for b in range(blocks):
            acc = None if ready else neighbours(slot, b, False)
            for i in range(zb):
                z = b * zb + i
                lap = (ACC[z] if ready else acc[i]) + centre * ref[n, z]
                value = carried(ref, n, z, whole_x, whole_y) + KP[z] * lap
                if z == at:
                    value = value + IV[z] * plane
                ref[n + 1, z] = value
                keep(slot ^ 1, z, value)

    for n in range(NF):
        advance(U, n + 1, n % 2, src_hot * (0.5 * amp_at(n)), src_depth, n == 0)
        if n == max(0, NF - 2):
            field_relay(L, 1, adj_state)

    for z in range(depth):
        illum = None
        for n in range(NF):
            value = U[n + 2, z, own_x, own_y]
            illum = value * value if illum is None else illum + value * value
        GI[1, z] = illum
    take(adj_state[1])
    for z in range(depth):
        keep(2, z, L[1, z], True)
    for b in range(blocks):
        ACC[b * zb : (b + 1) * zb] = neighbours(2, b, True)
    field_relay(L, 0, adjn_state)
    far_first = sorted(range(1, shots), key=lambda j: -min(j, shots - j))

    def to_owners(f):
        idx = group(GR.at[f])
        for j in far_first:
            put(idx, GI.at[f, pl.ds(peer("shots", j) * owned, owned)], GR.at[f, j - 1], {"shots": j})
        return idx

    illum_parts = to_owners(1)
    take(adjn_state[1])

    def plane_of(n):
        return 0.5 * (CNT[...] * U[n + 1, rec_depth] - OB[n - 1])

    for n in range(NF, 1, -1):
        advance(L, NF + 1 - n, 2 + (NF - n) % 2, plane_of(n), rec_depth, n == NF)

    last = NF
    for b in range(blocks):
        ACC[b * zb : (b + 1) * zb, :, 0:cols] = neighbours(2 + (NF - 1) % 2, b, False, own_y)
    SR[0] = plane_of(1)
    source_plane = SR[0, own_x, own_y]
    for z in range(depth):
        lap = ACC[z, own_x, 0:cols] + centre * L[last, z, own_x, own_y]
        lam = carried(L, last, z, own_x, own_y) + KP[z, own_x, own_y] * lap
        if z == rec_depth:
            lam = lam + IV[z, own_x, own_y] * source_plane
        u = [U[n, z, own_x, own_y] for n in range(NF + 2)]
        grad = lam * (u[2] - 2.0 * u[1] + u[0])
        for n in range(1, NF):
            grad = grad + L[NF + 1 - n, z, own_x, own_y] * (u[n + 2] - 2.0 * u[n + 1] + u[n])
        GI[0, z] = grad

    grad_parts = to_owners(0)
    plane = src_hot * (0.5 * amp_at(NF))
    for b in range(blocks):
        acc = neighbours(NF % 2, b, False)
        for i in range(zb):
            z = b * zb + i
            value = carried(U, NF + 1, z, whole_x, whole_y)
            if z == src_depth:
                value = value + IV[z] * plane
            U[NF + 2, z] = value
            ACC[z] = KP[z] * (acc[i] + centre * U[NF + 1, z])
    below = GI[1, pl.ds(s * owned, owned)] + floor_share * shots
    take(illum_parts)
    for j in range(1, shots):
        below = below + GR[1, j - 1]
    above = GI[0, pl.ds(s * owned, owned)]
    take(grad_parts)
    for j in range(1, shots):
        above = above + GR[0, j - 1]
    mine = above / below
    PC[pl.ds(s * owned, owned), own_x, own_y] = mine
    slab = in_slab(PC)
    own = slab(me, c)
    most = jnp.max(jnp.abs(mine), axis=0)
    most = functools.reduce(jnp.maximum, [most[r : r + reach] for r in range(0, rows, reach)])
    for i in range(1, dom):
        HS[i - 1, 0:owned] = jnp.where(peer("dom", i) > d, mine[:, rows - reach : rows], mine[:, 0:reach])
        HS[i - 1, owned] = most
    close = [j for j in range(1, shots) if min(j, shots - j) == 1]
    column = {}
    for members in (close, [j for j in far_first if j not in close]):
        if members:
            idx = group(PC.at[pl.ds(0, len(members) * owned), 0:rows, 0:cols])
            column[idx] = members
    which = {j: idx for idx, members in column.items() for j in members}
    beside, corner, cross = group(HR), group(CR), group(PC.at[:, 0:rows, far_cols])
    for j in far_first + [0]:
        if j:
            put(which[j], own, own, {"shots": j})
        for i in range(1, dom):
            put(beside, HS.at[i - 1], HR.at[i - 1, s], {"dom": i, "shots": j})
            for k in range(1, sub):
                put(corner, HS.at[i - 1, owned], CR.at[i - 1, k - 1, s], {"dom": i, "shots": j, "sub": k})
    put_sub(cross, own, own)
    for idx, members in column.items():
        take(idx)
        for j in members:
            here = slab({"shots": source("shots", j), "dom": d}, c)
            put_sub(cross, here, here)
    top = jnp.abs(PC[0, own_x, own_y])
    for z in range(1, depth):
        top = jnp.maximum(top, jnp.abs(PC[z, own_x, own_y]))
    take(cross)
    for k in range(1, sub):
        for z in range(depth):
            top = jnp.maximum(top, jnp.abs(PC[z, own_x, ys(source("sub", k))]))
    take(corner)
    take(beside)
    rest = None
    for i in range(1, dom):
        across = xs(source("dom", i))
        for j in range(shots):
            values = [HR[i - 1, j, owned]] + [CR[i - 1, k - 1, j] for k in range(1, sub)]
            for value in values:
                rest = value if rest is None else jnp.maximum(rest, value)
        for z in range(depth):
            halo = HR[i - 1, z // owned, z % owned]
            PC[z, across, own_y] = jnp.concatenate([halo] * (rows // reach), axis=0)
    top = jnp.concatenate([top, rest], axis=0)
    peak = jnp.max(jnp.max(top, axis=0, keepdims=True), axis=1, keepdims=True)
    scale = 1.0 / (peak + 1e-06)
    both_ref[0:owned] = mine * scale
    rate = step_rate * scale
    slot = (NF + 1) % 2
    for z in range(depth):
        factor = 1.0 - rate * PC[z]
        factor = factor * factor
        value = U[NF + 2, z] + ACC[z] * factor
        U[NF + 2, z] = value
        keep(slot, z, value)
    for b in range(blocks):
        ACC[b * zb : (b + 1) * zb, :, 0:cols] = neighbours(slot, b, False, own_y)
    SR[1] = src_hot * (0.5 * amp_at(NF + 1))
    for z in range(depth):
        lap = ACC[z, own_x, 0:cols] + centre * U[NF + 2, z, own_x, own_y]
        factor = 1.0 - rate * PC[z, own_x, own_y]
        value = carried(U, NF + 2, z, own_x, own_y) + KP[z, own_x, own_y] * (factor * factor) * lap
        if z == src_depth:
            value = value + IV[z, own_x, own_y] * SR[1, own_x, own_y]
        both_ref[owned + z] = value
    for idx in range(len(groups)):
        whole_group(idx).wait_send()


def part(both_ref, dir_ref, out_ref):
    owned = dir_ref.shape[0]
    dir_ref[...] = both_ref[0:owned]
    out_ref[0] = both_ref[owned:]


def solution(mesh):
    shots, dom, sub = mesh.shape["shots"], mesh.shape["dom"], mesh.shape["sub"]
    parts = mesh.shape["groups"]

    def shards(velocity, wave_prev, wave_now, adj_next, adj_now, sponge, wavelet, src_pos, rec_pos, observed):
        depth, rows, cols = sponge.shape
        owned = velocity.shape[0]
        X, Y = dom * rows, sub * cols
        zb = min(depth, max(1, 128 // X))
        ym = along_y(Y)
        zx = along_zx(zb, X)
        vm = pl.BlockSpec(memory_space=pltpu.VMEM)
        hbm = pl.BlockSpec(memory_space=pltpu.HBM)
        sm = pl.BlockSpec(memory_space=pltpu.SMEM)
        operands = (
            velocity, wave_prev, wave_now, adj_next, adj_now, sponge, wavelet, src_pos, rec_pos, observed,
            jnp.asarray(ym), jnp.asarray(zx),
        )
        whole = pltpu.VMEM((depth, X, Y), F32)
        sharing = max([n for n in (parts * shots, shots) if depth % n == 0], default=1)
        both = pl.pallas_call(
            functools.partial(kernel, (parts, shots, dom, sub, depth, rows, cols, owned, zb, sharing)),
            out_shape=jax.ShapeDtypeStruct((owned + depth, rows, cols), F32),
            in_specs=[sm if a.ndim == 1 else hbm for a in operands],
            out_specs=vm,
            scratch_shapes=[
                (pltpu.SMEM if a.size < 128 else pltpu.VMEM)(a.shape, a.dtype)
                for a in operands if a.ndim > 1 and a is not velocity and a is not sponge
            ] + [
                pltpu.VMEM((NF + 3, depth, X, Y), F32),
                pltpu.VMEM((NF + 1, depth, X, Y), F32),
                pltpu.VMEM((4, 2, depth + 2 * reach, X, Y), BF16),
                whole, pltpu.VMEM((depth, X, Y), jnp.int32), whole, whole, whole, whole,
                pltpu.VMEM((max(1, dom - 1), owned + 1, reach, cols), F32),
                pltpu.VMEM((max(1, dom - 1), shots, owned + 1, reach, cols), F32),
                pltpu.VMEM((max(1, dom - 1), max(1, sub - 1), shots, reach, cols), F32),
                pltpu.VMEM((NF, X, Y), F32),
                pltpu.VMEM((X, Y), F32),
                pltpu.VMEM((2, X, Y), F32),
                pltpu.VMEM((2, depth, rows, cols), F32),
                pltpu.VMEM((2, max(1, shots - 1), owned, rows, cols), F32),
                pltpu.SemaphoreType.DMA((N_SEMS,)),
                pltpu.SemaphoreType.DMA((N_SEMS,)),
                pltpu.SemaphoreType.DMA((len(operands) - 1,)),
            ],
            compiler_params=pltpu.CompilerParams(
                collective_id=0, has_side_effects=True, vmem_limit_bytes=VM_MAIN
            ),
        )(*(pltpu.with_memory_space_constraint(a, pltpu.HBM) if a.ndim > 1 else a for a in operands))
        return tuple(pl.pallas_call(
            part,
            out_shape=(
                jax.ShapeDtypeStruct((owned, rows, cols), F32),
                jax.ShapeDtypeStruct((1, depth, rows, cols), F32),
            ),
            in_specs=[vm],
            out_specs=(vm, vm),
            compiler_params=pltpu.CompilerParams(vmem_limit_bytes=VM_PART),
        )(both))

    return jax.shard_map(
        shards,
        mesh=mesh,
        in_specs=(
            P(("groups", "shots"), "dom", "sub"),
            P(("groups", "shots"), None, "dom", "sub"),
            P(("groups", "shots"), None, "dom", "sub"),
            P(("groups", "shots"), None, "dom", "sub"),
            P(("groups", "shots"), None, "dom", "sub"),
            P(None, "dom", "sub"),
            P(("groups", "shots"), None),
            P(("groups", "shots")),
            P(("groups", "shots"), None),
            P(("groups", "shots"), None, None),
        ),
        out_specs=(
            P(("groups", "shots"), "dom", "sub"),
            P(("groups", "shots"), None, "dom", "sub"),
        ),
        check_vma=False,
    )
```

```python
import functools

import jax
import jax.numpy as jnp
import numpy as np
from jax import lax
from jax.experimental import pallas as pl
from jax.experimental.pallas import tpu as pltpu
from jax.sharding import PartitionSpec as P

VM_MAIN = 48 * 1024 * 1024
VM_PART = 2 * 1024 * 1024
NF = 4
NFIN = 2

coeffs = (-205.0 / 72.0, 8.0 / 5.0, -1.0 / 5.0, 8.0 / 315.0, -1.0 / 560.0)
damp_rate = 0.2
step_rate = 0.1
floor_share = 0.5
src_depth = 2
rec_depth = 1
reach = 4
unit = coeffs[1]
centre = 3.0 * coeffs[0] / unit

MESH = pl.DeviceIdType.MESH
F32 = jnp.float32
BF16 = jnp.bfloat16


def along_y(size):
    full = np.zeros((size, size), np.float32)
    for row in range(size):
        for k in range(1, reach + 1):
            for col in (row - k, row + k):
                if 0 <= col < size:
                    full[row, col] = coeffs[k] / unit
    return full.astype(BF16)


def along_zx(zb, X):
    full = np.zeros((zb, X, zb + 2 * reach, X), np.float32)
    for z in range(zb):
        for x in range(X):
            for k in range(1, reach + 1):
                for other in (-k, k):
                    full[z, x, z + reach + other, x] = coeffs[k] / unit
                    if 0 <= x + other < X:
                        full[z, x, z + reach, x + other] = coeffs[k] / unit
    return full.reshape(zb * X, (zb + 2 * reach) * X).astype(BF16)


def split(value):
    high = value.astype(BF16)
    low = (value - high.astype(F32)).astype(BF16)
    return high, low


CHUNKS = 2
AHEAD = 2
N_SEMS = 20 + 2 * CHUNKS


def kernel(
    sizes,
    vel_in, prev_in, now_in, adjn_in, adj_in, sponge_in, amp_in, src_ref, rec_in, obs_in, ym_in, zx_in,
    both_ref,
    prev_ref, now_ref, adjn_ref, adj_ref, amp_ref, rec_ref, obs_ref, ym_ref, zx_ref,
    U, L, H, V, SP, IV, KP, ACC, PC, HS, HR, CR, OB, CNT, SR, GI, GR, ss, rs, ls,
):
    parts, shots, dom, sub, depth, rows, cols, owned, zb, sharing = sizes
    X, Y = dom * rows, sub * cols
    s = lax.axis_index("shots")
    d = lax.axis_index("dom")
    c = lax.axis_index("sub")
    g = lax.axis_index("groups")
    counts = {"groups": parts, "shots": shots, "dom": dom, "sub": sub}
    me = {"groups": g, "shots": s, "dom": d, "sub": c}
    groups = []

    def peer(axis, j):
        return lax.rem(me[axis] + j, counts[axis])

    def source(axis, j):
        return lax.rem(me[axis] + (counts[axis] - j), counts[axis])

    def xs(i):
        return pl.ds(pl.multiple_of(i * rows, rows), rows)

    def ys(i):
        return pl.ds(pl.multiple_of(i * cols, cols), cols)

    def group(total):
        groups.append(total)
        return len(groups) - 1

    def put(idx, src, dst, shifts):
        pltpu.make_async_remote_copy(
            src_ref=src, dst_ref=dst, send_sem=ss.at[idx], recv_sem=rs.at[idx],
            device_id={axis: peer(axis, j) for axis, j in shifts.items() if j}, device_id_type=MESH,
        ).start()

    def whole_group(idx):
        return pltpu.make_async_remote_copy(
            src_ref=groups[idx], dst_ref=groups[idx], send_sem=ss.at[idx], recv_sem=rs.at[idx],
            device_id={"sub": peer("sub", 1)}, device_id_type=MESH,
        )

    def take(idx):
        whole_group(idx).wait_recv()

    def put_sub(idx, src, dst):
        for k in range(1, sub):
            put(idx, src, dst, {"sub": k})

    far_cols, far_rows = pl.ds(0, (sub - 1) * cols), pl.ds(0, (dom - 1) * rows)

    def field_send(ref, n, lo=0, size=None):
        size = depth if size is None else size
        part_of = pl.ds(lo, size)
        state = group(ref.at[n, part_of, far_rows, 0:cols]), group(ref.at[n, part_of, :, far_cols])
        here = ref.at[n, part_of, xs(d), ys(c)]
        for i in range(1, dom):
            put(state[0], here, here, {"dom": i})
        put_sub(state[1], here, here)
        return state

    def field_relay(ref, n, state, lo=0, size=None):
        part_of = pl.ds(lo, depth if size is None else size)
        take(state[0])
        for i in range(1, dom):
            here = ref.at[n, part_of, xs(source("dom", i)), ys(c)]
            put_sub(state[1], here, here)

    def in_slab(ref):
        return lambda at, k: ref.at[pl.ds(at["shots"] * owned, owned), xs(at["dom"]), ys(k)]

    def neighbours(slot, b, exact, lanes=slice(None)):
        lo = b * zb
        acc = None
        for part_of in (0,) if exact else (0, 1):
            near = H[slot, part_of, pl.ds(lo, zb + 2 * reach), :, lanes].reshape((zb + 2 * reach) * X, -1)
            mid = H[slot, part_of, pl.ds(lo + reach, zb)].reshape(zb * X, Y)
            term = jnp.dot(zx_ref[...], near, preferred_element_type=F32)
            acc = term if acc is None else acc + term
            acc = acc + jnp.dot(mid, ym_ref[:, lanes], preferred_element_type=F32)
        return acc.reshape(zb, X, -1)

    def keep(slot, z, value, exact=False):
        high = value.astype(BF16)
        H[slot, 0, reach + z] = high
        if not exact:
            H[slot, 1, reach + z] = (value - high.astype(F32)).astype(BF16)

    def amp_at(n):
        return amp_ref[0, n]

    blocks = depth // zb
    barrier = pltpu.get_barrier_semaphore()
    greeted = 0
    shifts = [{"shots": j, "dom": i, "sub": k} for j in range(shots) for i in range(dom) for k in range(sub)][1:]
    sharers = [{"groups": i, "shots": j} for j in range(shots) for i in range(parts if sharing > shots else 1)][1:sharing]
    for shift in [shift for shift in sharers if shift["groups"]] + shifts:
        pl.semaphore_signal(
            barrier, inc=1, device_id={axis: peer(axis, j) for axis, j in shift.items() if j}, device_id_type=MESH
        )
        greeted += 1

    own_x, own_y = xs(d), ys(c)
    own_slab = in_slab(V)({"shots": s, "dom": d}, c)
    loads = []
    for source_ref, target in (
        (now_in, now_ref), (prev_in, prev_ref), (adj_in, adj_ref), (adjn_in, adjn_ref),
        (vel_in, own_slab), (sponge_in, SP.at[:, own_x, own_y]),
        (rec_in, rec_ref), (obs_in, obs_ref), (amp_in, amp_ref), (ym_in, ym_ref), (zx_in, zx_ref),
    ):
        loads.append(pltpu.make_async_copy(source_ref, target, ls.at[len(loads)]))
        loads[-1].start()

    pl.semaphore_wait(barrier, greeted)

    share = depth // sharing
    mine_at = pl.ds(pl.multiple_of((g * shots + s if sharing > shots else s) * share, share), share) if sharing > 1 else slice(None)
    slab = in_slab(V)
    vel_across = group(V.at[0:owned, far_rows, 0:cols])
    vel_near = group(V.at[pl.ds(0, (shots - 1) * owned), 0:rows, 0:cols])
    vel_far = group(V.at[pl.ds(0, (shots - 1) * owned), far_rows, 0:cols])
    vel_cross = group(V.at[:, :, far_cols])
    mask_across = group(SP.at[0:share, far_rows, 0:cols])
    mask_far = group(SP.at[pl.ds(0, (sharing - 1) * share), far_rows, 0:cols]) if sharing > 1 else None
    mask_cross = group(SP.at[:, :, far_cols])
    for i in range(1, dom):
        put(vel_across, vel_in, own_slab, {"dom": i})
        put(mask_across, sponge_in.at[mine_at], SP.at[mine_at, own_x, own_y], {"dom": i})
    for j in range(1, shots):
        put(vel_near, vel_in, own_slab, {"shots": j})
    loads[0].wait()
    U[1, :, own_x, own_y] = now_ref[0].astype(F32)
    now_state = field_send(U, 1)
    put_sub(vel_cross, vel_in, own_slab)
    put_sub(mask_cross, sponge_in, SP.at[:, own_x, own_y])
    loads[1].wait()
    U[0, :, own_x, own_y] = prev_ref[0].astype(F32)
    prev_state = field_send(U, 0)
    loads[2].wait()
    L[1, :, own_x, own_y] = adj_ref[0].astype(F32)
    adj_state = field_send(L, 1)
    loads[3].wait()
    L[0, :, own_x, own_y] = adjn_ref[0].astype(F32)
    chunks = CHUNKS if blocks % CHUNKS == 0 else 1
    long = depth // chunks
    adjn_state = [field_send(L, 0, i * long, long) for i in range(chunks)]
    for z in range(depth):
        PC[z] = jnp.zeros((X, Y), F32)
    for load in loads[4:]:
        load.wait()

    edge = jnp.zeros((reach, X, Y), BF16)
    for slot in range(H.shape[0]):
        for part_of in range(2):
            H[slot, part_of, 0:reach] = edge
            H[slot, part_of, reach + depth : 2 * reach + depth] = edge
    pos = rec_ref[...]
    row_of = jnp.zeros_like(pos)
    for x in range(1, X):
        row_of = row_of + (pos >= x * Y).astype(jnp.int32)
    col_of = pos - row_of * Y
    nrec = pos.shape[1]
    x_hot = (lax.broadcasted_iota(jnp.int32, (X, nrec), 0) == row_of).astype(F32)
    y_hot = (lax.broadcasted_iota(jnp.int32, (Y, nrec), 0) == col_of).astype(F32).astype(BF16)

    def spread(lhs):
        return lax.dot_general(lhs, y_hot, (((1,), (1,)), ((), ())), preferred_element_type=F32)

    CNT[...] = spread(x_hot.astype(BF16))
    take(vel_across)
    for i in range(1, dom):
        here = slab({"shots": s, "dom": source("dom", i)}, c)
        for j in range(1, shots):
            put(vel_far, here, here, {"shots": j})
        put_sub(vel_cross, here, here)
    take(mask_across)
    for i in range(1, dom):
        here = SP.at[mine_at, xs(source("dom", i)), own_y]
        for shift in sharers:
            put(mask_far, here, here, shift)
    take(vel_near)
    for j in range(1, shots):
        here = slab({"shots": source("shots", j), "dom": d}, c)
        put_sub(vel_cross, here, here)
    for n in range(NF):
        vals = x_hot * obs_ref[0, n : n + 1, :]
        a = vals.astype(BF16)
        b, rest = split(vals - a.astype(F32))
        OB[n] = spread(a) + spread(b) + spread(rest)
    flat = lax.broadcasted_iota(jnp.int32, (X, Y), 0) * Y + lax.broadcasted_iota(jnp.int32, (X, Y), 1)
    src_hot = (flat == src_ref[0]).astype(F32)

    field_relay(U, 1, now_state)
    take(now_state[1])
    for z in range(depth):
        keep(0, z, U[1, z], True)
    for b in range(blocks):
        ACC[b * zb : (b + 1) * zb] = neighbours(0, b, True)
    take(vel_far)
    for i in range(1, dom):
        for j in range(1, shots):
            here = slab({"shots": source("shots", j), "dom": source("dom", i)}, c)
            put_sub(vel_cross, here, here)
    field_relay(U, 0, prev_state)
    if sharing > 1:
        take(mask_far)
    for i in range(1, dom):
        here = SP.at[:, xs(source("dom", i)), own_y]
        put_sub(mask_cross, here, here)
    take(vel_cross)
    take(mask_cross)
    for z in range(depth):
        twice = 2.0 - (2.0 - 2.0 / (1.0 + damp_rate)) * SP[z].astype(F32)
        IV[z] = twice
        vel = V[z]
        KP[z] = vel * vel * (0.5 * unit * twice)
    take(prev_state[1])

    def carried(ref, n, z, xr, yr):
        before = ref[n - 1, z, xr, yr]
        return IV[z, xr, yr] * (ref[n, z, xr, yr] - before) + before

    whole_x, whole_y = slice(None), slice(None)

    def step(ref, n, slot, plane, at, b, ready):
        acc = None if ready else neighbours(slot, b, False)
        for i in range(zb):
            z = b * zb + i
            lap = (ACC[z] if ready else acc[i]) + centre * ref[n, z]
            value = carried(ref, n, z, whole_x, whole_y) + KP[z] * lap
            if z == at:
                value = value + IV[z] * plane()
            ref[n + 1, z] = value
            keep(slot ^ 1, z, value)

    for n in range(NF):
        for b in range(blocks):
            step(U, n + 1, n % 2, lambda: src_hot * (0.5 * amp_at(n)), src_depth, b, n == 0)
        if n == max(0, NF - 2):
            field_relay(L, 1, adj_state)

    for z in range(depth):
        illum = None
        for n in range(NF):
            value = U[n + 2, z, own_x, own_y]
            illum = value * value if illum is None else illum + value * value
        GI[1, z] = illum
    take(adj_state[1])
    for z in range(depth):
        keep(2, z, L[1, z], True)
    for b in range(blocks):
        ACC[b * zb : (b + 1) * zb] = neighbours(2, b, True)
    far_first = sorted(range(1, shots), key=lambda j: -min(j, shots - j))

    def to_owners(f):
        idx = group(GR.at[f])
        for j in far_first:
            put(idx, GI.at[f, pl.ds(peer("shots", j) * owned, owned)], GR.at[f, j - 1], {"shots": j})
        return idx

    illum_parts = to_owners(1)
    def plane_of(n):
        return 0.5 * (CNT[...] * U[n + 1, rec_depth] - OB[n - 1])

    last = NF

    def image(b):
        lo = b * zb
        ACC[pl.ds(lo, zb), :, 0:cols] = neighbours(2 + (NF - 1) % 2, b, False, own_y)
        for i in range(zb):
            z = lo + i
            lap = ACC[z, own_x, 0:cols] + centre * L[last, z, own_x, own_y]
            lam = carried(L, last, z, own_x, own_y) + KP[z, own_x, own_y] * lap
            if i == rec_depth % zb:
                here = jnp.where(z == rec_depth, 1.0, 0.0)
                lam = lam + here * (IV[z, own_x, own_y] * SR[0, own_x, own_y])
            u = [U[n, z, own_x, own_y] for n in range(NF + 2)]
            grad = lam * (u[2] - 2.0 * u[1] + u[0])
            for n in range(1, NF):
                grad = grad + L[NF + 1 - n, z, own_x, own_y] * (u[n + 2] - 2.0 * u[n + 1] + u[n])
            GI[0, z] = grad

    for chunk in range(chunks):
        for following in range(chunk, min(chunk + AHEAD, chunks)):
            if following >= chunk + AHEAD - 1 or chunk == 0:
                field_relay(L, 0, adjn_state[following], following * long, long)
        take(adjn_state[chunk][1])
        for b in range(chunk * blocks // chunks, (chunk + 1) * blocks // chunks):
            step(L, 1, 2, lambda: plane_of(NF), rec_depth, b, True)
    for q in range(1, NF - 1):
        for b in range(blocks):
            step(L, 1 + q, 2 + q % 2, lambda: plane_of(NF - q), rec_depth, b, False)
    SR[0] = plane_of(1)
    if owned == zb:
        grad_parts = group(GR.at[0])
        for j in far_first + [0]:
            image(peer("shots", j))
            if j:
                put(grad_parts, GI.at[0, pl.ds(peer("shots", j) * owned, owned)], GR.at[0, j - 1], {"shots": j})
    else:
        for b in range(blocks):
            image(b)
        grad_parts = to_owners(0)
    plane = src_hot * (0.5 * amp_at(NF))
    for b in range(blocks):
        acc = neighbours(NF % 2, b, False)
        for i in range(zb):
            z = b * zb + i
            value = carried(U, NF + 1, z, whole_x, whole_y)
            if z == src_depth:
                value = value + IV[z] * plane
            U[NF + 2, z] = value
            ACC[z] = KP[z] * (acc[i] + centre * U[NF + 1, z])
    below = GI[1, pl.ds(s * owned, owned)] + floor_share * shots
    take(illum_parts)
    for j in range(1, shots):
        below = below + GR[1, j - 1]
    above = GI[0, pl.ds(s * owned, owned)]
    take(grad_parts)
    for j in range(1, shots):
        above = above + GR[0, j - 1]
    mine = above / below
    PC[pl.ds(s * owned, owned), own_x, own_y] = mine
    slab = in_slab(PC)
    own = slab(me, c)
    most = jnp.max(jnp.abs(mine), axis=0)
    most = functools.reduce(jnp.maximum, [most[r : r + reach] for r in range(0, rows, reach)])
    for i in range(1, dom):
        HS[i - 1, 0:owned] = jnp.where(peer("dom", i) > d, mine[:, rows - reach : rows], mine[:, 0:reach])
        HS[i - 1, owned] = most
    close = [j for j in range(1, shots) if min(j, shots - j) == 1]
    column = {}
    for members in (close, [j for j in far_first if j not in close]):
        if members:
            idx = group(PC.at[pl.ds(0, len(members) * owned), 0:rows, 0:cols])
            column[idx] = members
    which = {j: idx for idx, members in column.items() for j in members}
    beside, corner, cross = group(HR), group(CR), group(PC.at[:, 0:rows, far_cols])
    for j in far_first + [0]:
        if j:
            put(which[j], own, own, {"shots": j})
        for i in range(1, dom):
            put(beside, HS.at[i - 1], HR.at[i - 1, s], {"dom": i, "shots": j})
            for k in range(1, sub):
                put(corner, HS.at[i - 1, owned], CR.at[i - 1, k - 1, s], {"dom": i, "shots": j, "sub": k})
    put_sub(cross, own, own)
    for idx, members in column.items():
        take(idx)
        for j in members:
            here = slab({"shots": source("shots", j), "dom": d}, c)
            put_sub(cross, here, here)
    top = jnp.abs(PC[0, own_x, own_y])
    for z in range(1, depth):
        top = jnp.maximum(top, jnp.abs(PC[z, own_x, own_y]))
    take(cross)
    for k in range(1, sub):
        for z in range(depth):
            top = jnp.maximum(top, jnp.abs(PC[z, own_x, ys(source("sub", k))]))
    take(corner)
    take(beside)
    rest = None
    for i in range(1, dom):
        across = xs(source("dom", i))
        for j in range(shots):
            values = [HR[i - 1, j, owned]] + [CR[i - 1, k - 1, j] for k in range(1, sub)]
            for value in values:
                rest = value if rest is None else jnp.maximum(rest, value)
        for z in range(depth):
            halo = HR[i - 1, z // owned, z % owned]
            PC[z, across, own_y] = jnp.concatenate([halo] * (rows // reach), axis=0)
    top = jnp.concatenate([top, rest], axis=0)
    peak = jnp.max(jnp.max(top, axis=0, keepdims=True), axis=1, keepdims=True)
    scale = 1.0 / (peak + 1e-06)
    both_ref[0:owned] = mine * scale
    rate = step_rate * scale
    slot = (NF + 1) % 2
    for z in range(depth):
        factor = 1.0 - rate * PC[z]
        factor = factor * factor
        value = U[NF + 2, z] + ACC[z] * factor
        U[NF + 2, z] = value
        keep(slot, z, value)
    for b in range(blocks):
        ACC[b * zb : (b + 1) * zb, :, 0:cols] = neighbours(slot, b, False, own_y)
    SR[1] = src_hot * (0.5 * amp_at(NF + 1))
    for z in range(depth):
        lap = ACC[z, own_x, 0:cols] + centre * U[NF + 2, z, own_x, own_y]
        factor = 1.0 - rate * PC[z, own_x, own_y]
        value = carried(U, NF + 2, z, own_x, own_y) + KP[z, own_x, own_y] * (factor * factor) * lap
        if z == src_depth:
            value = value + IV[z, own_x, own_y] * SR[1, own_x, own_y]
        both_ref[owned + z] = value
    for idx in range(len(groups)):
        whole_group(idx).wait_send()


def part(both_ref, dir_ref, out_ref, sems):
    owned, depth = dir_ref.shape[0], out_ref.shape[1]
    first = pltpu.make_async_copy(both_ref.at[pl.ds(0, owned)], dir_ref, sems.at[0])
    second = pltpu.make_async_copy(both_ref.at[pl.ds(owned, depth)], out_ref.at[0], sems.at[1])
    second.start()
    first.start()
    second.wait()
    first.wait()


def solution(mesh):
    shots, dom, sub = mesh.shape["shots"], mesh.shape["dom"], mesh.shape["sub"]
    parts = mesh.shape["groups"]

    def shards(velocity, wave_prev, wave_now, adj_next, adj_now, sponge, wavelet, src_pos, rec_pos, observed):
        depth, rows, cols = sponge.shape
        owned = velocity.shape[0]
        X, Y = dom * rows, sub * cols
        zb = min(depth, max(1, 128 // X))
        ym = along_y(Y)
        zx = along_zx(zb, X)
        vm = pl.BlockSpec(memory_space=pltpu.VMEM)
        hbm = pl.BlockSpec(memory_space=pltpu.HBM)
        sm = pl.BlockSpec(memory_space=pltpu.SMEM)
        operands = (
            velocity, wave_prev, wave_now, adj_next, adj_now, sponge, wavelet, src_pos, rec_pos, observed,
            jnp.asarray(ym), jnp.asarray(zx),
        )
        whole = pltpu.VMEM((depth, X, Y), F32)
        sharing = max([n for n in (parts * shots, shots) if depth % n == 0], default=1)
        both = pl.pallas_call(
            functools.partial(kernel, (parts, shots, dom, sub, depth, rows, cols, owned, zb, sharing)),
            out_shape=jax.ShapeDtypeStruct((owned + depth, rows, cols), F32),
            in_specs=[sm if a.ndim == 1 else hbm for a in operands],
            out_specs=vm,
            scratch_shapes=[
                (pltpu.SMEM if a.size < 128 else pltpu.VMEM)(a.shape, a.dtype)
                for a in operands if a.ndim > 1 and a is not velocity and a is not sponge
            ] + [
                pltpu.VMEM((NF + 3, depth, X, Y), F32),
                pltpu.VMEM((NF + 1, depth, X, Y), F32),
                pltpu.VMEM((4, 2, depth + 2 * reach, X, Y), BF16),
                whole, pltpu.VMEM((depth, X, Y), jnp.int32), whole, whole, whole, whole,
                pltpu.VMEM((max(1, dom - 1), owned + 1, reach, cols), F32),
                pltpu.VMEM((max(1, dom - 1), shots, owned + 1, reach, cols), F32),
                pltpu.VMEM((max(1, dom - 1), max(1, sub - 1), shots, reach, cols), F32),
                pltpu.VMEM((NF, X, Y), F32),
                pltpu.VMEM((X, Y), F32),
                pltpu.VMEM((2, X, Y), F32),
                pltpu.VMEM((2, depth, rows, cols), F32),
                pltpu.VMEM((2, max(1, shots - 1), owned, rows, cols), F32),
                pltpu.SemaphoreType.DMA((N_SEMS,)),
                pltpu.SemaphoreType.DMA((N_SEMS,)),
                pltpu.SemaphoreType.DMA((len(operands) - 1,)),
            ],
            compiler_params=pltpu.CompilerParams(
                collective_id=0, has_side_effects=True, vmem_limit_bytes=VM_MAIN
            ),
        )(*(pltpu.with_memory_space_constraint(a, pltpu.HBM) if a.ndim > 1 else a for a in operands))
        return tuple(pl.pallas_call(
            part,
            out_shape=(
                jax.ShapeDtypeStruct((owned, rows, cols), F32),
                jax.ShapeDtypeStruct((1, depth, rows, cols), F32),
            ),
            in_specs=[vm],
            out_specs=(pl.BlockSpec(memory_space=pl.ANY), pl.BlockSpec(memory_space=pl.ANY)),
            scratch_shapes=[pltpu.SemaphoreType.DMA((2,))],
            compiler_params=pltpu.CompilerParams(vmem_limit_bytes=VM_PART),
        )(both))

    return jax.shard_map(
        shards,
        mesh=mesh,
        in_specs=(
            P(("groups", "shots"), "dom", "sub"),
            P(("groups", "shots"), None, "dom", "sub"),
            P(("groups", "shots"), None, "dom", "sub"),
            P(("groups", "shots"), None, "dom", "sub"),
            P(("groups", "shots"), None, "dom", "sub"),
            P(None, "dom", "sub"),
            P(("groups", "shots"), None),
            P(("groups", "shots")),
            P(("groups", "shots"), None),
            P(("groups", "shots"), None, None),
        ),
        out_specs=(
            P(("groups", "shots"), "dom", "sub"),
            P(("groups", "shots"), None, "dom", "sub"),
        ),
        check_vma=False,
    )
```

```python
import functools

import jax
import jax.numpy as jnp
import numpy as np
from jax import lax
from jax.experimental import pallas as pl
from jax.experimental.pallas import tpu as pltpu
from jax.sharding import PartitionSpec as P

VM_MAIN = 48 * 1024 * 1024
VM_PART = 2 * 1024 * 1024
NF = 4
NFIN = 2

coeffs = (-205.0 / 72.0, 8.0 / 5.0, -1.0 / 5.0, 8.0 / 315.0, -1.0 / 560.0)
damp_rate = 0.2
step_rate = 0.1
floor_share = 0.5
src_depth = 2
rec_depth = 1
reach = 4
unit = coeffs[1]
centre = 3.0 * coeffs[0] / unit

MESH = pl.DeviceIdType.MESH
F32 = jnp.float32
BF16 = jnp.bfloat16


def along_y(size):
    full = np.zeros((size, size), np.float32)
    for row in range(size):
        for k in range(1, reach + 1):
            for col in (row - k, row + k):
                if 0 <= col < size:
                    full[row, col] = coeffs[k] / unit
    return full.astype(BF16)


def along_zx(zb, X):
    full = np.zeros((zb, X, zb + 2 * reach, X), np.float32)
    for z in range(zb):
        for x in range(X):
            for k in range(1, reach + 1):
                for other in (-k, k):
                    full[z, x, z + reach + other, x] = coeffs[k] / unit
                    if 0 <= x + other < X:
                        full[z, x, z + reach, x + other] = coeffs[k] / unit
    return full.reshape(zb * X, (zb + 2 * reach) * X).astype(BF16)


def split(value):
    high = value.astype(BF16)
    low = (value - high.astype(F32)).astype(BF16)
    return high, low


CHUNKS = 2
AHEAD = 2
N_SEMS = 19 + 2 * CHUNKS


def kernel(
    sizes,
    vel_in, prev_in, now_in, adjn_in, adj_in, sponge_in, amp_in, src_ref, rec_in, obs_in, ym_in, zx_in,
    both_ref,
    prev_ref, now_ref, adjn_ref, adj_ref, amp_ref, rec_ref, obs_ref, ym_ref, zx_ref,
    U, L, H, V, SP, IV, KP, ACC, PC, HS, HR, OB, CNT, SR, GI, GR, ss, rs, ls,
):
    parts, shots, dom, sub, depth, rows, cols, owned, zb, sharing = sizes
    X, Y = dom * rows, sub * cols
    s = lax.axis_index("shots")
    d = lax.axis_index("dom")
    c = lax.axis_index("sub")
    g = lax.axis_index("groups")
    counts = {"groups": parts, "shots": shots, "dom": dom, "sub": sub}
    me = {"groups": g, "shots": s, "dom": d, "sub": c}
    groups = []

    def peer(axis, j):
        return lax.rem(me[axis] + j, counts[axis])

    def source(axis, j):
        return lax.rem(me[axis] + (counts[axis] - j), counts[axis])

    def xs(i):
        return pl.ds(pl.multiple_of(i * rows, rows), rows)

    def ys(i):
        return pl.ds(pl.multiple_of(i * cols, cols), cols)

    def group(total):
        groups.append(total)
        return len(groups) - 1

    def put(idx, src, dst, shifts):
        pltpu.make_async_remote_copy(
            src_ref=src, dst_ref=dst, send_sem=ss.at[idx], recv_sem=rs.at[idx],
            device_id={axis: peer(axis, j) for axis, j in shifts.items() if j}, device_id_type=MESH,
        ).start()

    def whole_group(idx):
        return pltpu.make_async_remote_copy(
            src_ref=groups[idx], dst_ref=groups[idx], send_sem=ss.at[idx], recv_sem=rs.at[idx],
            device_id={"sub": peer("sub", 1)}, device_id_type=MESH,
        )

    def take(idx):
        whole_group(idx).wait_recv()

    def put_sub(idx, src, dst):
        for k in range(1, sub):
            put(idx, src, dst, {"sub": k})

    far_cols, far_rows = pl.ds(0, (sub - 1) * cols), pl.ds(0, (dom - 1) * rows)

    def field_send(ref, n, lo=0, size=None):
        size = depth if size is None else size
        part_of = pl.ds(lo, size)
        state = group(ref.at[n, part_of, far_rows, 0:cols]), group(ref.at[n, part_of, :, far_cols])
        here = ref.at[n, part_of, xs(d), ys(c)]
        for i in range(1, dom):
            put(state[0], here, here, {"dom": i})
        put_sub(state[1], here, here)
        return state

    def field_relay(ref, n, state, lo=0, size=None):
        part_of = pl.ds(lo, depth if size is None else size)
        take(state[0])
        for i in range(1, dom):
            here = ref.at[n, part_of, xs(source("dom", i)), ys(c)]
            put_sub(state[1], here, here)

    def in_slab(ref):
        return lambda at, k: ref.at[pl.ds(at["shots"] * owned, owned), xs(at["dom"]), ys(k)]

    def neighbours(slot, b, exact, lanes=slice(None)):
        lo = b * zb
        acc = None
        for part_of in (0,) if exact else (0, 1):
            near = H[slot, part_of, pl.ds(lo, zb + 2 * reach), :, lanes].reshape((zb + 2 * reach) * X, -1)
            mid = H[slot, part_of, pl.ds(lo + reach, zb)].reshape(zb * X, Y)
            term = jnp.dot(zx_ref[...], near, preferred_element_type=F32)
            acc = term if acc is None else acc + term
            acc = acc + jnp.dot(mid, ym_ref[:, lanes], preferred_element_type=F32)
        return acc.reshape(zb, X, -1)

    def keep(slot, z, value, exact=False):
        high = value.astype(BF16)
        H[slot, 0, reach + z] = high
        if not exact:
            H[slot, 1, reach + z] = (value - high.astype(F32)).astype(BF16)

    def amp_at(n):
        return amp_ref[0, n]

    blocks = depth // zb
    barrier = pltpu.get_barrier_semaphore()
    greeted = 0
    shifts = [{"shots": j, "dom": i, "sub": k} for j in range(shots) for i in range(dom) for k in range(sub)][1:]
    sharers = [{"groups": i, "shots": j} for j in range(shots) for i in range(parts if sharing > shots else 1)][1:sharing]
    shifts = [shift for shift in shifts if shift["dom"] or not (shift["shots"] and shift["sub"])]
    for shift in shifts + [shift for shift in sharers if shift["groups"]]:
        pl.semaphore_signal(
            barrier, inc=1, device_id={axis: peer(axis, j) for axis, j in shift.items() if j}, device_id_type=MESH
        )
        greeted += 1

    own_x, own_y = xs(d), ys(c)
    own_slab = in_slab(V)({"shots": s, "dom": d}, c)
    loads = []
    for source_ref, target in (
        (now_in, now_ref), (prev_in, prev_ref), (adj_in, adj_ref), (adjn_in, adjn_ref),
        (vel_in, own_slab), (sponge_in, SP.at[:, own_x, own_y]),
        (rec_in, rec_ref), (obs_in, obs_ref), (amp_in, amp_ref), (ym_in, ym_ref), (zx_in, zx_ref),
    ):
        loads.append(pltpu.make_async_copy(source_ref, target, ls.at[len(loads)]))
        loads[-1].start()

    pl.semaphore_wait(barrier, greeted)

    share = depth // sharing
    mine_at = pl.ds(pl.multiple_of((g * shots + s if sharing > shots else s) * share, share), share) if sharing > 1 else slice(None)
    slab = in_slab(V)
    vel_across = group(V.at[0:owned, far_rows, 0:cols])
    vel_near = group(V.at[pl.ds(0, (shots - 1) * owned), 0:rows, 0:cols])
    vel_far = group(V.at[pl.ds(0, (shots - 1) * owned), far_rows, 0:cols])
    vel_cross = group(V.at[:, :, far_cols])
    mask_across = group(SP.at[0:share, far_rows, 0:cols])
    mask_far = group(SP.at[pl.ds(0, (sharing - 1) * share), far_rows, 0:cols]) if sharing > 1 else None
    mask_cross = group(SP.at[:, :, far_cols])
    for i in range(1, dom):
        put(vel_across, vel_in, own_slab, {"dom": i})
        put(mask_across, sponge_in.at[mine_at], SP.at[mine_at, own_x, own_y], {"dom": i})
    for j in range(1, shots):
        put(vel_near, vel_in, own_slab, {"shots": j})
    loads[0].wait()
    U[1, :, own_x, own_y] = now_ref[0].astype(F32)
    now_state = field_send(U, 1)
    put_sub(vel_cross, vel_in, own_slab)
    put_sub(mask_cross, sponge_in, SP.at[:, own_x, own_y])
    loads[1].wait()
    U[0, :, own_x, own_y] = prev_ref[0].astype(F32)
    prev_state = field_send(U, 0)
    loads[2].wait()
    L[1, :, own_x, own_y] = adj_ref[0].astype(F32)
    adj_state = field_send(L, 1)
    loads[3].wait()
    L[0, :, own_x, own_y] = adjn_ref[0].astype(F32)
    chunks = CHUNKS if blocks % CHUNKS == 0 else 1
    long = depth // chunks
    adjn_state = [field_send(L, 0, i * long, long) for i in range(chunks)]
    for z in range(depth):
        PC[z] = jnp.zeros((X, Y), F32)
    for load in loads[4:]:
        load.wait()

    edge = jnp.zeros((reach, X, Y), BF16)
    for slot in range(H.shape[0]):
        for part_of in range(2):
            H[slot, part_of, 0:reach] = edge
            H[slot, part_of, reach + depth : 2 * reach + depth] = edge
    pos = rec_ref[...]
    row_of = jnp.zeros_like(pos)
    for x in range(1, X):
        row_of = row_of + (pos >= x * Y).astype(jnp.int32)
    col_of = pos - row_of * Y
    nrec = pos.shape[1]
    x_hot = (lax.broadcasted_iota(jnp.int32, (X, nrec), 0) == row_of).astype(F32)
    y_hot = (lax.broadcasted_iota(jnp.int32, (Y, nrec), 0) == col_of).astype(F32).astype(BF16)

    def spread(lhs):
        return lax.dot_general(lhs, y_hot, (((1,), (1,)), ((), ())), preferred_element_type=F32)

    CNT[...] = spread(x_hot.astype(BF16))
    take(vel_across)
    for i in range(1, dom):
        here = slab({"shots": s, "dom": source("dom", i)}, c)
        for j in range(1, shots):
            put(vel_far, here, here, {"shots": j})
        put_sub(vel_cross, here, here)
    take(mask_across)
    for i in range(1, dom):
        here = SP.at[mine_at, xs(source("dom", i)), own_y]
        for shift in sharers:
            put(mask_far, here, here, shift)
    take(vel_near)
    for j in range(1, shots):
        here = slab({"shots": source("shots", j), "dom": d}, c)
        put_sub(vel_cross, here, here)
    for n in range(NF):
        vals = x_hot * obs_ref[0, n : n + 1, :]
        a = vals.astype(BF16)
        b, rest = split(vals - a.astype(F32))
        OB[n] = spread(a) + spread(b) + spread(rest)
    flat = lax.broadcasted_iota(jnp.int32, (X, Y), 0) * Y + lax.broadcasted_iota(jnp.int32, (X, Y), 1)
    src_hot = (flat == src_ref[0]).astype(F32)

    field_relay(U, 1, now_state)
    take(now_state[1])
    for z in range(depth):
        keep(0, z, U[1, z], True)
    for b in range(blocks):
        ACC[b * zb : (b + 1) * zb] = neighbours(0, b, True)
    take(vel_far)
    for i in range(1, dom):
        for j in range(1, shots):
            here = slab({"shots": source("shots", j), "dom": source("dom", i)}, c)
            put_sub(vel_cross, here, here)
    field_relay(U, 0, prev_state)
    if sharing > 1:
        take(mask_far)
    for i in range(1, dom):
        here = SP.at[:, xs(source("dom", i)), own_y]
        put_sub(mask_cross, here, here)
    take(vel_cross)
    take(mask_cross)
    for z in range(depth):
        twice = 2.0 - (2.0 - 2.0 / (1.0 + damp_rate)) * SP[z].astype(F32)
        IV[z] = twice
        vel = V[z]
        KP[z] = vel * vel * (0.5 * unit * twice)
    take(prev_state[1])

    def carried(ref, n, z, xr, yr):
        before = ref[n - 1, z, xr, yr]
        return IV[z, xr, yr] * (ref[n, z, xr, yr] - before) + before

    whole_x, whole_y = slice(None), slice(None)

    def step(ref, n, slot, plane, at, b, ready):
        acc = None if ready else neighbours(slot, b, False)
        for i in range(zb):
            z = b * zb + i
            lap = (ACC[z] if ready else acc[i]) + centre * ref[n, z]
            value = carried(ref, n, z, whole_x, whole_y) + KP[z] * lap
            if z == at:
                value = value + IV[z] * plane()
            ref[n + 1, z] = value
            keep(slot ^ 1, z, value)

    for n in range(NF):
        for b in range(blocks):
            step(U, n + 1, n % 2, lambda: src_hot * (0.5 * amp_at(n)), src_depth, b, n == 0)
        if n == max(0, NF - 2):
            field_relay(L, 1, adj_state)

    for z in range(depth):
        illum = None
        for n in range(NF):
            value = U[n + 2, z, own_x, own_y]
            illum = value * value if illum is None else illum + value * value
        GI[1, z] = illum
    take(adj_state[1])
    for z in range(depth):
        keep(2, z, L[1, z], True)
    for b in range(blocks):
        ACC[b * zb : (b + 1) * zb] = neighbours(2, b, True)
    far_first = sorted(range(1, shots), key=lambda j: -min(j, shots - j))

    def to_owners(f):
        idx = group(GR.at[f])
        for j in far_first:
            put(idx, GI.at[f, pl.ds(peer("shots", j) * owned, owned)], GR.at[f, j - 1], {"shots": j})
        return idx

    illum_parts = to_owners(1)
    def plane_of(n):
        return 0.5 * (CNT[...] * U[n + 1, rec_depth] - OB[n - 1])

    last = NF

    def image(b):
        lo = b * zb
        ACC[pl.ds(lo, zb), :, 0:cols] = neighbours(2 + (NF - 1) % 2, b, False, own_y)
        for i in range(zb):
            z = lo + i
            lap = ACC[z, own_x, 0:cols] + centre * L[last, z, own_x, own_y]
            lam = carried(L, last, z, own_x, own_y) + KP[z, own_x, own_y] * lap
            if i == rec_depth % zb:
                here = jnp.where(z == rec_depth, 1.0, 0.0)
                lam = lam + here * (IV[z, own_x, own_y] * SR[0, own_x, own_y])
            u = [U[n, z, own_x, own_y] for n in range(NF + 2)]
            grad = lam * (u[2] - 2.0 * u[1] + u[0])
            for n in range(1, NF):
                grad = grad + L[NF + 1 - n, z, own_x, own_y] * (u[n + 2] - 2.0 * u[n + 1] + u[n])
            GI[0, z] = grad

    for chunk in range(chunks):
        for following in range(chunk, min(chunk + AHEAD, chunks)):
            if following >= chunk + AHEAD - 1 or chunk == 0:
                field_relay(L, 0, adjn_state[following], following * long, long)
        take(adjn_state[chunk][1])
        for b in range(chunk * blocks // chunks, (chunk + 1) * blocks // chunks):
            step(L, 1, 2, lambda: plane_of(NF), rec_depth, b, True)
    for q in range(1, NF - 1):
        for b in range(blocks):
            step(L, 1 + q, 2 + q % 2, lambda: plane_of(NF - q), rec_depth, b, False)
    SR[0] = plane_of(1)
    if owned == zb:
        grad_parts = group(GR.at[0])
        for j in far_first + [0]:
            image(peer("shots", j))
            if j:
                put(grad_parts, GI.at[0, pl.ds(peer("shots", j) * owned, owned)], GR.at[0, j - 1], {"shots": j})
    else:
        for b in range(blocks):
            image(b)
        grad_parts = to_owners(0)
    plane = src_hot * (0.5 * amp_at(NF))
    for b in range(blocks):
        acc = neighbours(NF % 2, b, False)
        for i in range(zb):
            z = b * zb + i
            value = carried(U, NF + 1, z, whole_x, whole_y)
            if z == src_depth:
                value = value + IV[z] * plane
            U[NF + 2, z] = value
            ACC[z] = KP[z] * (acc[i] + centre * U[NF + 1, z])
    below = GI[1, pl.ds(s * owned, owned)] + floor_share * shots
    take(illum_parts)
    for j in range(1, shots):
        below = below + GR[1, j - 1]
    above = GI[0, pl.ds(s * owned, owned)]
    take(grad_parts)
    for j in range(1, shots):
        above = above + GR[0, j - 1]
    mine = above / below
    PC[pl.ds(s * owned, owned), own_x, own_y] = mine
    slab = in_slab(PC)
    own = slab(me, c)
    most = jnp.max(jnp.abs(mine), axis=0)
    most = functools.reduce(jnp.maximum, [most[r : r + reach] for r in range(0, rows, reach)])
    for i in range(1, dom):
        HS[i - 1, 0:owned] = jnp.where(peer("dom", i) > d, mine[:, rows - reach : rows], mine[:, 0:reach])
        HS[i - 1, owned] = most
    close = [j for j in range(1, shots) if min(j, shots - j) == 1]
    column = {}
    for members in (close, [j for j in far_first if j not in close]):
        if members:
            idx = group(PC.at[pl.ds(0, len(members) * owned), 0:rows, 0:cols])
            column[idx] = members
    which = {j: idx for idx, members in column.items() for j in members}
    beside, cross = group(HR), group(PC.at[:, 0:rows, far_cols])
    for j in far_first + [0]:
        if j:
            put(which[j], own, own, {"shots": j})
        for i in range(1, dom):
            put(beside, HS.at[i - 1], HR.at[i - 1, s, 0 : owned + 1], {"dom": i, "shots": j})
            for k in range(1, sub):
                put(beside, HS.at[i - 1, owned], HR.at[i - 1, s, owned + k], {"dom": i, "shots": j, "sub": k})
    put_sub(cross, own, own)
    for idx, members in column.items():
        take(idx)
        for j in members:
            here = slab({"shots": source("shots", j), "dom": d}, c)
            put_sub(cross, here, here)
    top = jnp.abs(PC[0, own_x, own_y])
    for z in range(1, depth):
        top = jnp.maximum(top, jnp.abs(PC[z, own_x, own_y]))
    take(cross)
    for k in range(1, sub):
        for z in range(depth):
            top = jnp.maximum(top, jnp.abs(PC[z, own_x, ys(source("sub", k))]))
    take(beside)
    rest = None
    for i in range(1, dom):
        across = xs(source("dom", i))
        for j in range(shots):
            values = [HR[i - 1, j, owned + k] for k in range(sub)]
            for value in values:
                rest = value if rest is None else jnp.maximum(rest, value)
        for z in range(depth):
            halo = HR[i - 1, z // owned, z % owned]
            PC[z, across, own_y] = jnp.concatenate([halo] * (rows // reach), axis=0)
    top = jnp.concatenate([top, rest], axis=0)
    peak = jnp.max(jnp.max(top, axis=0, keepdims=True), axis=1, keepdims=True)
    scale = 1.0 / (peak + 1e-06)
    both_ref[0:owned] = mine * scale
    rate = step_rate * scale
    slot = (NF + 1) % 2
    for z in range(depth):
        factor = 1.0 - rate * PC[z]
        factor = factor * factor
        value = U[NF + 2, z] + ACC[z] * factor
        U[NF + 2, z] = value
        keep(slot, z, value)
    for b in range(blocks):
        ACC[b * zb : (b + 1) * zb, :, 0:cols] = neighbours(slot, b, False, own_y)
    SR[1] = src_hot * (0.5 * amp_at(NF + 1))
    for z in range(depth):
        lap = ACC[z, own_x, 0:cols] + centre * U[NF + 2, z, own_x, own_y]
        factor = 1.0 - rate * PC[z, own_x, own_y]
        value = carried(U, NF + 2, z, own_x, own_y) + KP[z, own_x, own_y] * (factor * factor) * lap
        if z == src_depth:
            value = value + IV[z, own_x, own_y] * SR[1, own_x, own_y]
        both_ref[owned + z] = value
    for idx in range(len(groups)):
        whole_group(idx).wait_send()


def part(both_ref, dir_ref, out_ref, sems):
    owned, depth = dir_ref.shape[0], out_ref.shape[1]
    first = pltpu.make_async_copy(both_ref.at[pl.ds(0, owned)], dir_ref, sems.at[0])
    second = pltpu.make_async_copy(both_ref.at[pl.ds(owned, depth)], out_ref.at[0], sems.at[1])
    second.start()
    first.start()
    second.wait()
    first.wait()


def solution(mesh):
    shots, dom, sub = mesh.shape["shots"], mesh.shape["dom"], mesh.shape["sub"]
    parts = mesh.shape["groups"]

    def shards(velocity, wave_prev, wave_now, adj_next, adj_now, sponge, wavelet, src_pos, rec_pos, observed):
        depth, rows, cols = sponge.shape
        owned = velocity.shape[0]
        X, Y = dom * rows, sub * cols
        zb = min(depth, max(1, 128 // X))
        ym = along_y(Y)
        zx = along_zx(zb, X)
        vm = pl.BlockSpec(memory_space=pltpu.VMEM)
        hbm = pl.BlockSpec(memory_space=pltpu.HBM)
        sm = pl.BlockSpec(memory_space=pltpu.SMEM)
        operands = (
            velocity, wave_prev, wave_now, adj_next, adj_now, sponge, wavelet, src_pos, rec_pos, observed,
            jnp.asarray(ym), jnp.asarray(zx),
        )
        whole = pltpu.VMEM((depth, X, Y), F32)
        sharing = max([n for n in (parts * shots, shots) if depth % n == 0], default=1)
        both = pl.pallas_call(
            functools.partial(kernel, (parts, shots, dom, sub, depth, rows, cols, owned, zb, sharing)),
            out_shape=jax.ShapeDtypeStruct((owned + depth, rows, cols), F32),
            in_specs=[sm if a.ndim == 1 else hbm for a in operands],
            out_specs=vm,
            scratch_shapes=[
                (pltpu.SMEM if a.size < 128 else pltpu.VMEM)(a.shape, a.dtype)
                for a in operands if a.ndim > 1 and a is not velocity and a is not sponge
            ] + [
                pltpu.VMEM((NF + 3, depth, X, Y), F32),
                pltpu.VMEM((NF + 1, depth, X, Y), F32),
                pltpu.VMEM((4, 2, depth + 2 * reach, X, Y), BF16),
                whole, pltpu.VMEM((depth, X, Y), jnp.int32), whole, whole, whole, whole,
                pltpu.VMEM((max(1, dom - 1), owned + 1, reach, cols), F32),
                pltpu.VMEM((max(1, dom - 1), shots, owned + sub, reach, cols), F32),
                pltpu.VMEM((NF, X, Y), F32),
                pltpu.VMEM((X, Y), F32),
                pltpu.VMEM((2, X, Y), F32),
                pltpu.VMEM((2, depth, rows, cols), F32),
                pltpu.VMEM((2, max(1, shots - 1), owned, rows, cols), F32),
                pltpu.SemaphoreType.DMA((N_SEMS,)),
                pltpu.SemaphoreType.DMA((N_SEMS,)),
                pltpu.SemaphoreType.DMA((len(operands) - 1,)),
            ],
            compiler_params=pltpu.CompilerParams(
                collective_id=0, has_side_effects=True, vmem_limit_bytes=VM_MAIN
            ),
        )(*(pltpu.with_memory_space_constraint(a, pltpu.HBM) if a.ndim > 1 else a for a in operands))
        return tuple(pl.pallas_call(
            part,
            out_shape=(
                jax.ShapeDtypeStruct((owned, rows, cols), F32),
                jax.ShapeDtypeStruct((1, depth, rows, cols), F32),
            ),
            in_specs=[vm],
            out_specs=(pl.BlockSpec(memory_space=pl.ANY), pl.BlockSpec(memory_space=pl.ANY)),
            scratch_shapes=[pltpu.SemaphoreType.DMA((2,))],
            compiler_params=pltpu.CompilerParams(vmem_limit_bytes=VM_PART),
        )(both))

    return jax.shard_map(
        shards,
        mesh=mesh,
        in_specs=(
            P(("groups", "shots"), "dom", "sub"),
            P(("groups", "shots"), None, "dom", "sub"),
            P(("groups", "shots"), None, "dom", "sub"),
            P(("groups", "shots"), None, "dom", "sub"),
            P(("groups", "shots"), None, "dom", "sub"),
            P(None, "dom", "sub"),
            P(("groups", "shots"), None),
            P(("groups", "shots")),
            P(("groups", "shots"), None),
            P(("groups", "shots"), None, None),
        ),
        out_specs=(
            P(("groups", "shots"), "dom", "sub"),
            P(("groups", "shots"), None, "dom", "sub"),
        ),
        check_vma=False,
    )
```
